512 devices in a mesh: expert: 16 (over z), shard: 32 (over y, x, core).
Axes of the slice: x: 4, y: 4, z: 16, core: 2. Of those that a mesh axis runs over, the one named last changes fastest.
Arguments:
- tokens: bfloat16 [384, 6144], P('expert', 'shard'), may hold values from -6 to 6
- routes: int32 [384, 2], P('expert'), may hold values from 0 to 7, all different within a row; in each aligned block of 24 rows (0 to 23, 24 to 47, ...) at most 12 rows name the same one
- w_router: bfloat16 [6144, 8], replicated, may hold values from -0.078125 to 0.078125
- w_gate: bfloat16 [6144, 65536], P(None, ('expert', 'shard')), may hold values from -0.078125 to 0.078125
- w_up: bfloat16 [6144, 65536], P(None, ('expert', 'shard')), may hold values from -0.078125 to 0.078125
- w_down: bfloat16 [65536, 6144], P(('expert', 'shard')), may hold values from -0.25 to 0.25
Outputs:
- mixed: bfloat16 [384, 6144], P('expert', 'shard')
The draws below stay inside these ranges and needn't reach their ends.
Inputs may be any that keep to these rules, and one draw needn't show every extreme that they name: `routes`: the two experts of a row differ; within each aligned block of 24 rows no expert is named more than 24 / 2 times, and some expert is named exactly that often.
All inputs are finite; a program needn't handle non-finite values.
Results may differ from the reference program's by a relative error of at most 0.017.
Values may be sent and summed in bfloat16 or wider, within the bound.
No kernel may reach another device: no remote copies, remote signals or barrier semaphores. Data moves between devices by JAX's collectives and lax.ppermute only.
A program may use at most 128 MiB of HBM per device.

```python
import math
import jax
import jax.numpy as jnp
import numpy as np
from jax import lax

D = 6144
EXPERTS = 8
FF_W = 8192
TOK_DEV = 24
TOKENS = 384
N_EXPERT = 16
N_SHARD = 32


def strengthened(drawn, stream_key, source, target, blocks, factor):
    def block_of(dim):
        return (jnp.arange(drawn.shape[dim]) // (drawn.shape[dim] // blocks)).reshape((-1,) + (1,) * (drawn.ndim - 1 - dim))

    first = jax.random.permutation(stream_key, blocks)[block_of(target)]
    second = (block_of(target) + blocks // 2) % blocks
    return jnp.where((block_of(source) == first) | (block_of(source) == second), factor * drawn, drawn)


def block_scale(own_key, dims, shards, low, high):
    loudness, own = 1.0, jax.random.fold_in(own_key, 6)
    for dim, shards_of in shards:
        draws = jnp.exp(jax.random.uniform(jax.random.fold_in(own, dim), (shards_of,), jnp.float32, low / len(shards), high / len(shards)))
        loudness = loudness * jnp.repeat(draws, dims[dim] // shards_of).reshape([-1 if axis == dim else 1 for axis in range(len(dims))])
    return loudness


def assign_block(rng, own, number, rows, number_of, top, bound, lean):
    sequence = jax.random.permutation(rng, number_of)
    heavy_load, usual = shares(number_of, rows * top, bound, lean, True), shares(number_of, rows * top, bound, lean, False)
    places = jnp.arange(number_of)

    def named(sizes, offset_by):
        used = int((sizes > 0).sum())
        fixed = max(1, used // 4)
        moved = fixed + (places - fixed + offset_by * (used - fixed)) % max(1, number_of - fixed)
        return jnp.zeros((number_of,), jnp.int32).at[sequence[jnp.where(places < fixed, places, moved)]].set(jnp.asarray(sizes, jnp.int32))

    sizes = jnp.where(number % 4 == 0, named(heavy_load, number // 4), named(usual, number - number // 4 - 1))
    mixed = jax.random.permutation(jax.random.fold_in(own, 3), number_of)
    source_of, sink = mixed[0:number_of // 2 * 2:2], mixed[1:number_of // 2 * 2:2]
    margin = jnp.minimum(sizes[source_of] - 1, bound - sizes[sink]) // 2
    margin = jnp.where((source_of == sequence[0]) | (sink == sequence[0]) | (sizes[sink] == 0), 0, jnp.maximum(margin, 0))
    moved = jax.random.randint(jax.random.fold_in(own, 4), (number_of // 2,), 0, 1 << 20) % (margin + 1)
    sizes = sizes.at[source_of].add(-moved).at[sink].add(moved)
    items = jnp.searchsorted(jnp.cumsum(sizes), jnp.arange(rows * top), side="right").astype(jnp.int32)
    table = items.reshape(top, rows).T
    table = table[jax.random.permutation(jax.random.fold_in(own, 1), rows)]
    offset_by = jax.random.randint(jax.random.fold_in(own, 2), (rows, 1), 0, top)
    return jnp.take_along_axis(table, (jnp.arange(top)[None, :] + offset_by) % top, axis=1)


def shares(number_of, total, most, skew, full):
    portions = [(1 << 20) // math.isqrt(rank ** skew) + 1 for rank in range(1, number_of + 1)]
    largest = most if full else min(most, max(-(-total // number_of), total * portions[0] // sum(portions)))
    least = 1 if total - largest >= number_of - 1 else 0
    counts, surplus = [largest] + [least] * (number_of - 1), total - largest - least * (number_of - 1)
    while surplus > 0:
        free = [i for i in range(1, number_of) if counts[i] < largest] or [i for i in range(1, number_of) if counts[i] < most]
        whole, left = sum([portions[i] for i in free]), surplus
        for i in free:
            addition = min(most - counts[i], max(1, left * portions[i] // whole), surplus)
            counts[i] = counts[i] + addition
            surplus = surplus - addition
    return np.array(counts)


def gaussian(rng, extent, scale, bound, split=(), held_as=jnp.bfloat16):
    drawn = jax.random.normal(rng, extent, jnp.float32) * scale
    if len(split) > 0:
        drawn = block_scale(rng, extent, split, -0.22, 0.18) * drawn
    return jnp.clip(drawn, min=-bound, max=bound).astype(held_as)


def heavy_noise(own_key, dims, spread, limit, split, heavy, held_as=jnp.bfloat16):
    entries = spread * jax.random.normal(own_key, dims, jnp.float32)
    if split:
        entries = entries * block_scale(own_key, dims, split, -0.22, 0.18)
    return jnp.clip(strengthened(entries, jax.random.fold_in(own_key, 3), *heavy), -limit, limit).astype(held_as)


def setup_inputs(seed: int = 0) -> dict:
    arg_keys = jax.random.split(jax.random.key(seed), 7)
    tokens = gaussian(arg_keys[0], (TOKENS, D), 1.0, 6.0, ((0, 16), (1, 32)))
    routes_keys = jax.random.split(jax.random.fold_in(arg_keys[1], 1), TOKENS // TOK_DEV)
    routes_turns = jax.random.permutation(jax.random.fold_in(arg_keys[1], 3), TOKENS // TOK_DEV)
    routes = jax.vmap(lambda own, number: assign_block(jax.random.fold_in(arg_keys[1], 2), own, number, TOK_DEV, EXPERTS, 2, TOK_DEV // 2, 2))(routes_keys, routes_turns).reshape((TOKENS, 2))
    w_router = gaussian(arg_keys[2], (D, EXPERTS), D ** -0.5, 0.078125)
    w_gate = gaussian(arg_keys[3], (D, EXPERTS * FF_W), D ** -0.5, 0.078125, ((1, 512),))
    w_up = gaussian(arg_keys[4], (D, EXPERTS * FF_W), D ** -0.5, 0.078125, ((1, 512),))
    w_down = heavy_noise(arg_keys[5], (EXPERTS * FF_W, D), FF_W ** -0.5, 0.25, ((0, 512),), (0, 1, 512, 6.0))
    return dict(tokens=tokens, routes=routes, w_router=w_router, w_gate=w_gate, w_up=w_up, w_down=w_down)


def pair_weights(logits, routes):
    picks = jnp.sum(jnp.where(routes[:, :, None] == jnp.arange(EXPERTS)[None, None, :], logits[:, None, :], 0.0), axis=2)
    first = 1.0 / (1.0 + jnp.exp(picks[:, 1] - picks[:, 0]))
    second = 1.0 / (1.0 + jnp.exp(picks[:, 0] - picks[:, 1]))
    return jnp.stack([first, second], axis=1)


def reference(tokens, routes, w_router, w_gate, w_up, w_down):
    logits = jnp.dot(tokens, w_router, preferred_element_type=jnp.float32)
    weights = pair_weights(logits, routes)
    repeat = max(1, N_EXPERT // EXPERTS)
    width = EXPERTS * FF_W // (N_EXPERT * N_SHARD)
    blocks = FF_W // (repeat * width)
    rows_most = N_EXPERT * (TOK_DEV // 2)
    mixed = jnp.zeros((TOKENS, D), jnp.float32)
    for expert in range(EXPERTS):
        hit = routes == expert
        coef = jnp.sum(jnp.where(hit, weights, 0.0), axis=1)
        routed = jnp.any(hit, axis=1)
        index = jnp.nonzero(routed, size=rows_most, fill_value=0)[0].astype(jnp.int32)
        valid = jnp.arange(rows_most) < jnp.sum(routed.astype(jnp.int32))
        chosen = tokens[index]
        low = expert * FF_W
        gate = jnp.dot(chosen, w_gate[:, low:low + FF_W], preferred_element_type=jnp.float32)
        up = jnp.dot(chosen, w_up[:, low:low + FF_W], preferred_element_type=jnp.float32)
        hidden = (jax.nn.silu(gate) * up).astype(jnp.bfloat16)
        hidden_blocks = hidden.reshape(rows_most, repeat * blocks, width)
        down_blocks = w_down[low:low + FF_W].reshape(repeat * blocks, width, D)
        total = jnp.zeros((rows_most, D), jnp.float32)
        for part in range(repeat):
            def add_block(step, acc):
                which = part * blocks + step
                left = lax.dynamic_index_in_dim(hidden_blocks, which, 1, keepdims=False)
                right = lax.dynamic_index_in_dim(down_blocks, which, 0, keepdims=False)
                term = jnp.dot(left, right, preferred_element_type=jnp.float32).astype(jnp.bfloat16)
                return acc + lax.optimization_barrier(term).astype(jnp.float32)
            part_sum = lax.fori_loop(0, blocks, add_block, jnp.zeros((rows_most, D), jnp.float32))
            rounded = lax.optimization_barrier(part_sum.astype(jnp.bfloat16))
            total = total + rounded.astype(jnp.float32)
        contrib = jnp.where(valid[:, None], coef[index][:, None] * total, 0.0)
        mixed = mixed.at[index].add(contrib)
    return mixed.astype(jnp.bfloat16)
```

```python
import jax
import jax.numpy as jnp
from jax import lax
from jax.experimental import pallas as pl
from jax.experimental.pallas import tpu as pltpu
from jax.sharding import Mesh, PartitionSpec as P

EXPERTS = 8
CAP = 12
HALF = 6
PLANES = 16
CHIPS = 16
ROWS = PLANES * HALF
TOK = 24
FEAT = 192
PAIR = 384
D = 6144
PADR = 8
LANES = 256
F32 = jnp.float32
BF16 = jnp.bfloat16
VM = pltpu.VMEM


def vmem():
    return pl.BlockSpec(memory_space=pltpu.VMEM)


def smem():
    return pl.BlockSpec(memory_space=pltpu.SMEM)


def iota(shape, dim):
    return lax.broadcasted_iota(jnp.int32, shape, dim)


def dot_nt(a, b):
    return lax.dot_general(a, b, (((1,), (1,)), ((), ())), preferred_element_type=F32)


def dot_tn(a, b):
    return lax.dot_general(a, b, (((0,), (0,)), ((), ())), preferred_element_type=F32)


def dot_nn(a, b):
    return jnp.dot(a, b, preferred_element_type=F32)


def dispatch_kernel(core_ref, routes_ref, tok_ref, out_ref, place_ref):
    core = core_ref[0]
    total = 2 * PLANES * PADR
    first = routes_ref[0:1, :]
    second = routes_ref[1:2, :]
    k8 = iota((EXPERTS, TOK), 0)
    named = ((k8 == first) | (k8 == second)).astype(F32)
    earlier = (iota((TOK, TOK), 0) < iota((TOK, TOK), 1)).astype(BF16)
    rank = dot_nn(named.astype(BF16), earlier)
    row = iota((total, EXPERTS), 0)
    pick = ((row >> 5) == iota((total, EXPERTS), 1)).astype(BF16)
    named_row = dot_nn(pick, named.astype(BF16))
    rank_row = dot_nn(pick, rank.astype(BF16))
    r = iota((total, TOK), 0)
    slot = (r & 7) + HALF * ((r >> 3) & 1)
    hit = (named_row > 0.5) & (rank_row == slot.astype(F32)) & ((r & 7) < HALF)
    place = hit.astype(F32).astype(BF16)
    place_ref[...] = place
    tok = tok_ref[...].astype(F32)
    wide = jnp.concatenate([tok, jnp.zeros((TOK, LANES - FEAT), F32)], axis=1)
    shifted = jnp.concatenate([jnp.zeros((TOK, LANES - FEAT), F32), tok], axis=1)
    wide = jnp.where(core == 0, wide, shifted).astype(BF16)
    lane = iota((LANES, TOK), 0) - jnp.where(core == 0, FEAT, 0)
    info = ((lane == first) | (lane == second)).astype(F32).astype(BF16)
    payload = dot_nn(place, wide) + dot_nt(place, info)
    out_ref[...] = payload.reshape(2 * PLANES, PADR, LANES).astype(BF16)


def repack_kernel(in_ref, out_ref, info_ref):
    x = in_ref[...].astype(F32).reshape(PLANES, 2, PADR, LANES)
    low = x[:, 0].reshape(PLANES * PADR, LANES).astype(BF16)
    high = x[:, 1].reshape(PLANES * PADR, LANES).astype(BF16)
    p = iota((ROWS, PLANES * PADR), 0)
    home = (p * 43) >> 8
    keep = (iota((ROWS, PLANES * PADR), 1) == p + 2 * home).astype(F32).astype(BF16)
    a = dot_nn(keep, low)
    b = dot_nn(keep, high)
    left = iota((ROWS, 128), 1) < 64
    middle = jnp.where(left, a[:, 128:], b[:, :128])
    block = jnp.concatenate([a[:, :128], middle, b[:, 128:]], axis=1).astype(BF16)
    for chip in range(CHIPS):
        out_ref[chip] = block
    info_ref[...] = a[:, 128:]


def expert_kernel(
    expert_ref, x_ref, info_ref, router_ref, gate_a, gate_b, up_a, up_b, down_a, down_b, out_ref
):
    expert = expert_ref[0]
    gate = jnp.zeros((ROWS, 256), F32)
    up = jnp.zeros((ROWS, 256), F32)
    logits = jnp.zeros((ROWS, EXPERTS), F32)
    for chip in range(CHIPS):
        rows = slice(chip * PAIR, (chip + 1) * PAIR)
        x = x_ref[chip]
        gate = gate + dot_nn(x, jnp.concatenate([gate_a[rows, :], gate_b[rows, :]], axis=1))
        up = up + dot_nn(x, jnp.concatenate([up_a[rows, :], up_b[rows, :]], axis=1))
        logits = logits + dot_nt(x, router_ref[:, rows])
    k = iota((ROWS, EXPERTS), 1)
    named = info_ref[:, 64 : 64 + EXPERTS]
    other = jnp.sum(jnp.where((k != expert) & (named > 0.5), logits, 0.0), axis=1, keepdims=True)
    own = jnp.sum(jnp.where(k == expert, logits, 0.0), axis=1, keepdims=True)
    weight = 1.0 / (1.0 + jnp.exp(other - own))
    hidden = (gate / (1.0 + jnp.exp(-gate)) * up * weight).astype(BF16)
    for chip in range(CHIPS):
        cols = slice(chip * PAIR, (chip + 1) * PAIR)
        down = jnp.concatenate([down_a[:, cols], down_b[:, cols]], axis=0)
        out_ref[chip] = dot_nn(hidden, down).astype(BF16)


def share_kernel(in_ref, out_ref):
    total = in_ref[0].astype(F32)
    for chip in range(1, CHIPS):
        total = total + in_ref[chip].astype(F32)
    total = total.astype(BF16)
    p = iota((PLANES * PADR, ROWS), 1)
    home = (p * 43) >> 8
    put = (iota((PLANES * PADR, ROWS), 0) == p + 2 * home).astype(F32).astype(BF16)
    spread = dot_nn(put, total).reshape(PLANES, PADR, PAIR)
    low = spread[:, :, :256].reshape(PLANES, 1, PADR, LANES)
    high = spread[:, :, 128:].reshape(PLANES, 1, PADR, LANES)
    both = jnp.concatenate([low, high], axis=1)
    out_ref[...] = both.reshape(2 * PLANES, PADR, LANES).astype(BF16)


def combine_kernel(core_ref, place_ref, in_ref, out_ref):
    core = core_ref[0]
    x = in_ref[...].astype(F32).reshape(2 * PLANES * PADR, LANES).astype(BF16)
    mixed = dot_tn(place_ref[...], x)
    out_ref[...] = jnp.where(core == 0, mixed[:, :FEAT], mixed[:, LANES - FEAT :]).astype(BF16)


def local(tokens, routes, w_router, w_gate, w_up, w_down):
    core = lax.axis_index("c").reshape(1).astype(jnp.int32)
    expert = (lax.axis_index("z") // (PLANES // EXPERTS)).reshape(1).astype(jnp.int32)
    swap = [(0, 1), (1, 0)]
    gate_b = lax.ppermute(w_gate, "c", swap)
    up_b = lax.ppermute(w_up, "c", swap)
    down_b = lax.ppermute(w_down, "c", swap)
    payload, place = pl.pallas_call(
        dispatch_kernel,
        out_shape=(
            jax.ShapeDtypeStruct((2 * PLANES, PADR, LANES), BF16),
            jax.ShapeDtypeStruct((2 * PLANES * PADR, TOK), BF16),
        ),
        in_specs=[smem(), vmem(), vmem()],
        out_specs=(vmem(), vmem()),
        name="dispatch",
    )(core, routes.T, tokens)
    arrived = lax.all_to_all(payload, ("z", "c"), 0, 0, tiled=True)
    blocks, info = pl.pallas_call(
        repack_kernel,
        out_shape=(
            jax.ShapeDtypeStruct((CHIPS, ROWS, PAIR), BF16),
            jax.ShapeDtypeStruct((ROWS, 128), F32),
        ),
        in_specs=[vmem()],
        out_specs=(vmem(), vmem()),
        name="repack",
    )(arrived)
    gathered = lax.all_to_all(blocks, ("y", "x"), 0, 0, tiled=True)
    terms = pl.pallas_call(
        expert_kernel,
        out_shape=jax.ShapeDtypeStruct((CHIPS, ROWS, PAIR), BF16),
        in_specs=[smem()] + [vmem()] * 9,
        out_specs=vmem(),
        compiler_params=pltpu.CompilerParams(vmem_limit_bytes=24 << 20),
        name="expert",
    )(expert, gathered, info, w_router.T, w_gate, gate_b, w_up, up_b, w_down, down_b)
    parts = lax.all_to_all(terms, ("y", "x"), 0, 0, tiled=True)
    shares = pl.pallas_call(
        share_kernel,
        out_shape=jax.ShapeDtypeStruct((2 * PLANES, PADR, LANES), BF16),
        in_specs=[vmem()],
        out_specs=vmem(),
        name="share",
    )(parts)
    back = lax.all_to_all(shares, ("z", "c"), 0, 0, tiled=True)
    return pl.pallas_call(
        combine_kernel,
        out_shape=jax.ShapeDtypeStruct((TOK, FEAT), BF16),
        in_specs=[smem(), vmem(), vmem()],
        out_specs=vmem(),
        name="combine",
    )(core, place, back)


def solution(mesh):
    fine = Mesh(mesh.devices.reshape(16, 4, 4, 2), ("z", "y", "x", "c"))
    shard = ("y", "x", "c")
    both = ("z",) + shard
    return jax.shard_map(
        local,
        mesh=fine,
        in_specs=(P("z", shard), P("z", None), P(), P(None, both), P(None, both), P(both, None)),
        out_specs=P("z", shard),
        check_vma=False,
    )
```

```python
import jax
import jax.numpy as jnp
from jax import lax
from jax.experimental import pallas as pl
from jax.experimental.pallas import tpu as pltpu
from jax.sharding import Mesh, PartitionSpec as P

EXPERTS = 8
HALF = 6
PLANES = 16
CHIPS = 16
ROWS = PLANES * HALF
TOK = 24
FEAT = 192
PAIR = 384
D = 6144
PAY = 24
PAYS = PLANES * PAY
UNITS = 256
PACK = ROWS + ROWS // 2
PER = 4
GROUPS = CHIPS // PER
GROUP = PER * PAIR
F32 = jnp.float32
BF16 = jnp.bfloat16


def vmem():
    return pl.BlockSpec(memory_space=pltpu.VMEM)


def smem():
    return pl.BlockSpec(memory_space=pltpu.SMEM)


def hbm():
    return pl.BlockSpec(memory_space=pltpu.HBM)


def anyspace():
    return pl.BlockSpec(memory_space=pl.ANY)


def small():
    return pltpu.CompilerParams(vmem_limit_bytes=8 << 20)


def iota(shape, dim):
    return lax.broadcasted_iota(jnp.int32, shape, dim)


def onehot(mask):
    return mask.astype(F32).astype(BF16)


def dot_nt(a, b):
    return lax.dot_general(a, b, (((1,), (1,)), ((), ())), preferred_element_type=F32)


def dot_tn(a, b):
    return lax.dot_general(a, b, (((0,), (0,)), ((), ())), preferred_element_type=F32)


def dot_nn(a, b):
    return jnp.dot(a, b, preferred_element_type=F32)


def ranks(routes_ref):
    first = routes_ref[0:1, :]
    second = routes_ref[1:2, :]
    k8 = iota((EXPERTS, TOK), 0)
    named = onehot((k8 == first) | (k8 == second))
    earlier = onehot(iota((TOK, TOK), 0) < iota((TOK, TOK), 1))
    rank = dot_nn(named, earlier)
    rank = jnp.where(named.astype(F32) > 0.5, rank, 100.0).astype(BF16)
    plane = iota((PLANES, PAY, EXPERTS), 0).reshape(PAYS, EXPERTS)
    pick = onehot((plane >> 1) == iota((PAYS, EXPERTS), 1))
    rank_row = dot_nn(pick, rank)
    i = iota((PLANES, PAY, TOK), 1).reshape(PAYS, TOK)
    return rank_row, i


def dispatch_kernel(core_ref, routes_ref, tok_ref, out_ref):
    core = core_ref[0]
    rank_row, i = ranks(routes_ref)
    first = routes_ref[0:1, :]
    second = routes_ref[1:2, :]
    is_a = i < 12
    is_b = (i >= 12) & (i < 18)
    slot = jnp.where(is_a, i, jnp.where(is_b, i - 12, i - 18))
    hit_low = rank_row == slot.astype(F32)
    hit_high = (rank_row == (slot + HALF).astype(F32)) & (i >= 12)
    tok = tok_ref[...].astype(F32)
    zero = jnp.zeros((TOK, 64), F32)
    part_a = jnp.where(core == 0, tok[:, :128], tok[:, 64:]).astype(BF16)
    head = jnp.concatenate([tok[:, :64], zero], axis=1)
    tail = jnp.concatenate([tok[:, 128:], zero], axis=1)
    part_b = jnp.where(core == 0, tail, head)
    part_b_high = pltpu.roll(part_b, 64, 1).astype(BF16)
    part_b = part_b.astype(BF16)
    lane = iota((128, TOK), 0)
    marks = onehot((lane == first) | (lane == second))
    marks_high = onehot((lane - 64 == first) | (lane - 64 == second))
    payload = dot_nn(onehot(hit_low & is_a), part_a)
    payload = payload + dot_nn(onehot(hit_low & is_b), part_b)
    payload = payload + dot_nn(onehot(hit_high & is_b), part_b_high)
    payload = payload + dot_nt(onehot(hit_low & (i >= 18)), marks)
    payload = payload + dot_nt(onehot(hit_high & (i >= 18)), marks_high)
    out_ref[...] = payload.reshape(PLANES, PAY, 128).astype(BF16)


def place_kernel(routes_ref, out_ref):
    rank_row, i = ranks(routes_ref)
    low = rank_row == (i - 12).astype(F32)
    high = rank_row == (i - 12 + HALF).astype(F32)
    inside = (i >= 12) & (i < 18)
    out_ref[0] = onehot((rank_row == i.astype(F32)) & (i < 12))
    out_ref[1] = onehot(low & inside)
    out_ref[2] = onehot(high & inside)


def repack_kernel(core_ref, in_ref, out_ref, info_ref, block_ref, sem):
    core = core_ref[0]
    x = in_ref[...].astype(F32).reshape(PAYS, 128).astype(BF16)
    p = iota((ROWS, PAYS), 0)
    at = iota((ROWS, PAYS), 1) - p - (PAY - HALF) * ((p * 43) >> 8)
    rest = dot_nn(onehot(at == 12), x)
    near = rest[: ROWS // 2]
    far = rest[ROWS // 2 :]
    left = (iota((ROWS // 2, 128), 1) < 64) == (core == 0)
    near_roll = pltpu.roll(near, 64, 1)
    far_roll = pltpu.roll(far, 64, 1)
    even_near = jnp.where(core == 0, near, near_roll)
    even_far = jnp.where(core == 0, far_roll, far)
    odd_near = jnp.where(core == 0, near_roll, near)
    odd_far = jnp.where(core == 0, far, far_roll)
    block_ref[0, :ROWS] = dot_nn(onehot(at == 0), x).astype(BF16)
    block_ref[0, ROWS:] = jnp.where(left, even_near, even_far).astype(BF16)
    copies = [
        pltpu.make_async_copy(block_ref.at[n % 2], out_ref.at[n], sem.at[n])
        for n in range(2 * CHIPS)
    ]
    for copy in copies[0::2]:
        copy.start()
    block_ref[1, :ROWS] = dot_nn(onehot(at == HALF), x).astype(BF16)
    block_ref[1, ROWS:] = jnp.where(left, odd_near, odd_far).astype(BF16)
    for copy in copies[1::2]:
        copy.start()
    info = dot_nn(onehot(at == 18), x)
    info_ref[...] = jnp.where(core == 0, info, pltpu.roll(info, 64, 1))
    for copy in copies:
        copy.wait()


def expert_kernel(
    expert_ref, x_ref, info_ref, router_ref, gate_a, gate_b, up_a, up_b, down_a, down_b,
    out_ref, wide_ref, down_ref, wide_sem, down_sem,
):
    expert = expert_ref[0]
    wide_copies = []
    down_copies = []
    for g in range(GROUPS):
        rows = pl.ds(g * GROUP, GROUP)
        for n, src in enumerate((gate_a, gate_b, up_a, up_b)):
            wide_copies.append(
                pltpu.make_async_copy(src.at[rows, :], wide_ref.at[n, rows, :], wide_sem.at[g, n])
            )
    for g in range(GROUPS):
        cols = pl.ds(g * GROUP, GROUP)
        for n, src in enumerate((down_a, down_b)):
            down_copies.append(
                pltpu.make_async_copy(
                    src.at[:, cols], down_ref.at[pl.ds(128 * n, 128), cols], down_sem.at[g, n]
                )
            )
    for copy in wide_copies + down_copies:
        copy.start()
    left = iota((ROWS // 2, 128), 1) < 64
    xs = []
    logits = jnp.zeros((ROWS, EXPERTS), F32)
    for g in range(GROUPS):
        parts = []
        for chip in range(g * PER, (g + 1) * PER):
            rest_a = x_ref[2 * chip, ROWS:].astype(F32)
            rest_b = x_ref[2 * chip + 1, ROWS:].astype(F32)
            near = jnp.where(left, rest_a, rest_b)
            far = pltpu.roll(jnp.where(left, rest_b, rest_a), 64, 1)
            middle = jnp.concatenate([near, far], axis=0).astype(BF16)
            parts += [x_ref[2 * chip, :ROWS], middle, x_ref[2 * chip + 1, :ROWS]]
        x = jnp.concatenate(parts, axis=1)
        xs.append(x)
        logits = logits + dot_nt(x, router_ref[:, g * GROUP : (g + 1) * GROUP])
    k = iota((ROWS, EXPERTS), 1)
    named = info_ref[:, :EXPERTS]
    other = jnp.sum(jnp.where((k != expert) & (named > 0.5), logits, 0.0), axis=1, keepdims=True)
    own = jnp.sum(jnp.where(k == expert, logits, 0.0), axis=1, keepdims=True)
    weight = 1.0 / (1.0 + jnp.exp(other - own))
    gate = jnp.zeros((ROWS, UNITS), F32)
    up = jnp.zeros((ROWS, UNITS), F32)
    for g in range(GROUPS):
        for n in range(4):
            wide_copies[g * 4 + n].wait()
        rows = slice(g * GROUP, (g + 1) * GROUP)
        x = xs[g]
        gate = gate + dot_nn(x, jnp.concatenate([wide_ref[0, rows, :], wide_ref[1, rows, :]], axis=1))
        up = up + dot_nn(x, jnp.concatenate([wide_ref[2, rows, :], wide_ref[3, rows, :]], axis=1))
    hidden = (gate / (1.0 + jnp.exp(-gate)) * up * weight).astype(BF16)
    for g in range(GROUPS):
        for n in range(2):
            down_copies[g * 2 + n].wait()
        terms = dot_nn(hidden, down_ref[:, g * GROUP : (g + 1) * GROUP])
        for n in range(PER):
            chip = g * PER + n
            base = n * PAIR
            near = terms[: ROWS // 2, base + 128 : base + 256]
            far = pltpu.roll(terms[ROWS // 2 :, base + 128 : base + 256], 64, 1)
            out_ref[2 * chip, :ROWS] = terms[:, base : base + 128].astype(BF16)
            out_ref[2 * chip, ROWS:] = jnp.where(left, near, far).astype(BF16)
            out_ref[2 * chip + 1, :ROWS] = terms[:, base + 256 : base + 384].astype(BF16)
            out_ref[2 * chip + 1, ROWS:] = jnp.where(left, far, near).astype(BF16)


def share_kernel(core_ref, in_ref, out_ref):
    core = core_ref[0]
    halves = []
    for half in range(2):
        total = in_ref[half].astype(F32)
        for chip in range(1, CHIPS):
            total = total + in_ref[2 * chip + half].astype(F32)
        halves.append(total)
    even = halves[0][ROWS:]
    odd = halves[1][ROWS:]
    left = iota((ROWS // 2, 128), 1) < 64
    low = jnp.where(left, even, pltpu.roll(odd, 64, 1))
    high = jnp.where(left, pltpu.roll(even, 64, 1), odd)
    near = jnp.where(core == 0, low, high)
    far = jnp.where(core == 0, high, low)
    rest = jnp.concatenate([near, far], axis=0).astype(BF16)
    p = iota((PAYS, ROWS), 1)
    at = iota((PAYS, ROWS), 0) - p - (PAY - HALF) * ((p * 43) >> 8)
    spread = dot_nn(onehot(at == 0), halves[0][:ROWS].astype(BF16))
    spread = spread + dot_nn(onehot(at == HALF), halves[1][:ROWS].astype(BF16))
    spread = spread + dot_nn(onehot(at == 2 * HALF), rest)
    out_ref[...] = spread.reshape(PLANES, PAY, 128).astype(BF16)


def combine_kernel(core_ref, place_ref, in_ref, out_ref):
    core = core_ref[0]
    x = in_ref[...].astype(F32).reshape(PAYS, 128).astype(BF16)
    side = dot_tn(place_ref[0], x)
    low = dot_tn(place_ref[1], x)
    high = pltpu.roll(dot_tn(place_ref[2], x), 64, 1)
    rest = (low + high)[:, :64]
    even = jnp.concatenate([side, rest], axis=1)
    odd = jnp.concatenate([rest, side], axis=1)
    out_ref[...] = jnp.where(core == 0, even, odd).astype(BF16)


def local(tokens, routes, w_router, w_gate, w_up, w_down):
    core = lax.axis_index("c").reshape(1).astype(jnp.int32)
    expert = (lax.axis_index("z") >> 1).reshape(1).astype(jnp.int32)
    swap = [(0, 1), (1, 0)]
    routes_t = routes.T
    payload = pl.pallas_call(
        dispatch_kernel,
        out_shape=jax.ShapeDtypeStruct((PLANES, PAY, 128), BF16),
        in_specs=[smem(), vmem(), vmem()],
        out_specs=vmem(),
        name="dispatch",
    )(core, routes_t, tokens)
    gate_b = lax.ppermute(w_gate, "c", swap)
    up_b = lax.ppermute(w_up, "c", swap)
    down_b = lax.ppermute(w_down, "c", swap)
    place = pl.pallas_call(
        place_kernel,
        out_shape=jax.ShapeDtypeStruct((3, PAYS, TOK), BF16),
        in_specs=[vmem()],
        out_specs=vmem(),
        name="place",
    )(routes_t)
    arrived = lax.all_to_all(payload, "z", 0, 0, tiled=True)
    blocks, info = pl.pallas_call(
        repack_kernel,
        out_shape=(
            jax.ShapeDtypeStruct((2 * CHIPS, PACK, 128), BF16),
            jax.ShapeDtypeStruct((ROWS, 128), F32),
        ),
        in_specs=[smem(), vmem()],
        out_specs=(anyspace(), vmem()),
        scratch_shapes=[pltpu.VMEM((2, PACK, 128), BF16), pltpu.SemaphoreType.DMA((2 * CHIPS,))],
        cost_estimate=pl.CostEstimate(flops=100000000000, transcendentals=0, bytes_accessed=1048576),
        name="repack",
    )(core, arrived)
    gathered = lax.all_to_all(blocks, ("y", "x", "c"), 0, 0, tiled=True)
    terms = pl.pallas_call(
        expert_kernel,
        out_shape=jax.ShapeDtypeStruct((2 * CHIPS, PACK, 128), BF16),
        in_specs=[smem()] + [vmem()] * 3 + [hbm()] * 6,
        out_specs=vmem(),
        scratch_shapes=[
            pltpu.VMEM((4, D, 128), BF16),
            pltpu.VMEM((UNITS, D), BF16),
            pltpu.SemaphoreType.DMA((GROUPS, 4)),
            pltpu.SemaphoreType.DMA((GROUPS, 2)),
        ],
        compiler_params=pltpu.CompilerParams(vmem_limit_bytes=48 << 20),
        name="expert",
    )(expert, gathered, info, w_router.T, w_gate, gate_b, w_up, up_b, w_down, down_b)
    parts = lax.all_to_all(terms, ("y", "x", "c"), 0, 0, tiled=True)
    shares = pl.pallas_call(
        share_kernel,
        out_shape=jax.ShapeDtypeStruct((PLANES, PAY, 128), BF16),
        in_specs=[smem(), vmem()],
        out_specs=vmem(),
        compiler_params=small(),
        name="share",
    )(core, parts)
    back = lax.all_to_all(shares, "z", 0, 0, tiled=True)
    return pl.pallas_call(
        combine_kernel,
        out_shape=jax.ShapeDtypeStruct((TOK, FEAT), BF16),
        in_specs=[smem(), vmem(), vmem()],
        out_specs=vmem(),
        compiler_params=small(),
        name="combine",
    )(core, place, back)


def solution(mesh):
    fine = Mesh(mesh.devices.reshape(16, 4, 4, 2), ("z", "y", "x", "c"))
    shard = ("y", "x", "c")
    both = ("z",) + shard
    return jax.shard_map(
        local,
        mesh=fine,
        in_specs=(P("z", shard), P("z", None), P(), P(None, both), P(None, both), P(both, None)),
        out_specs=P("z", shard),
        check_vma=False,
    )
```

```python
import jax
import jax.numpy as jnp
from jax import lax
from jax.experimental import pallas as pl
from jax.experimental.pallas import tpu as pltpu
from jax.sharding import Mesh, PartitionSpec as P

EXPERTS = 8
HALF = 6
PLANES = 16
CHIPS = 16
ROWS = PLANES * HALF
TOK = 24
FEAT = 192
PAIR = 384
D = 6144
PAY = 24
PAYS = PLANES * PAY
UNITS = 256
PACK = ROWS + ROWS // 2
PER = 16
GROUPS = CHIPS // PER
GROUP = PER * PAIR
F32 = jnp.float32
BF16 = jnp.bfloat16


def vmem():
    return pl.BlockSpec(memory_space=pltpu.VMEM)


def smem():
    return pl.BlockSpec(memory_space=pltpu.SMEM)


def hbm():
    return pl.BlockSpec(memory_space=pltpu.HBM)


def anyspace():
    return pl.BlockSpec(memory_space=pl.ANY)


def small():
    return pltpu.CompilerParams(vmem_limit_bytes=8 << 20)


def iota(shape, dim):
    return lax.broadcasted_iota(jnp.int32, shape, dim)


def onehot(mask):
    return mask.astype(F32).astype(BF16)


def dot_nt(a, b):
    return lax.dot_general(a, b, (((1,), (1,)), ((), ())), preferred_element_type=F32)


def dot_tn(a, b):
    return lax.dot_general(a, b, (((0,), (0,)), ((), ())), preferred_element_type=F32)


def dot_nn(a, b):
    return jnp.dot(a, b, preferred_element_type=F32)


def ranks(routes_ref):
    first = routes_ref[0:1, :]
    second = routes_ref[1:2, :]
    k8 = iota((EXPERTS, TOK), 0)
    named = onehot((k8 == first) | (k8 == second))
    earlier = onehot(iota((TOK, TOK), 0) < iota((TOK, TOK), 1))
    rank = dot_nn(named, earlier)
    rank = jnp.where(named.astype(F32) > 0.5, rank, 100.0).astype(BF16)
    plane = iota((PLANES, PAY, EXPERTS), 0).reshape(PAYS, EXPERTS)
    pick = onehot((plane >> 1) == iota((PAYS, EXPERTS), 1))
    rank_row = dot_nn(pick, rank)
    i = iota((PLANES, PAY, TOK), 1).reshape(PAYS, TOK)
    return rank_row, i


def dispatch_kernel(routes_ref, tok_ref, out_ref):
    core = lax.axis_index("c")
    rank_row, i = ranks(routes_ref)
    first = routes_ref[0:1, :]
    second = routes_ref[1:2, :]
    is_a = i < 12
    is_b = (i >= 12) & (i < 18)
    slot = jnp.where(is_a, i, jnp.where(is_b, i - 12, i - 18))
    hit_low = rank_row == slot.astype(F32)
    hit_high = (rank_row == (slot + HALF).astype(F32)) & (i >= 12)
    tok = tok_ref[...].astype(F32)
    zero = jnp.zeros((TOK, 64), F32)
    part_a = jnp.where(core == 0, tok[:, :128], tok[:, 64:]).astype(BF16)
    head = jnp.concatenate([tok[:, :64], zero], axis=1)
    tail = jnp.concatenate([tok[:, 128:], zero], axis=1)
    part_b = jnp.where(core == 0, tail, head)
    part_b_high = pltpu.roll(part_b, 64, 1).astype(BF16)
    part_b = part_b.astype(BF16)
    lane = iota((128, TOK), 0)
    marks = onehot((lane == first) | (lane == second))
    marks_high = onehot((lane - 64 == first) | (lane - 64 == second))
    payload = dot_nn(onehot(hit_low & is_a), part_a)
    payload = payload + dot_nn(onehot(hit_low & is_b), part_b)
    payload = payload + dot_nn(onehot(hit_high & is_b), part_b_high)
    payload = payload + dot_nt(onehot(hit_low & (i >= 18)), marks)
    payload = payload + dot_nt(onehot(hit_high & (i >= 18)), marks_high)
    out_ref[...] = payload.reshape(PLANES, PAY, 128).astype(BF16)


def place_kernel(routes_ref, out_ref):
    rank_row, i = ranks(routes_ref)
    low = rank_row == (i - 12).astype(F32)
    high = rank_row == (i - 12 + HALF).astype(F32)
    inside = (i >= 12) & (i < 18)
    out_ref[0] = onehot((rank_row == i.astype(F32)) & (i < 12))
    out_ref[1] = onehot(low & inside)
    out_ref[2] = onehot(high & inside)


def repack_kernel(in_ref, out_ref, info_ref):
    core = lax.axis_index("c")
    x = in_ref[...].astype(F32).reshape(PAYS, 128).astype(BF16)
    p = iota((ROWS, PAYS), 0)
    at = iota((ROWS, PAYS), 1) - p - (PAY - HALF) * ((p * 43) >> 8)
    rest = dot_nn(onehot(at == 12), x)
    near = rest[: ROWS // 2]
    far = rest[ROWS // 2 :]
    left = (iota((ROWS // 2, 128), 1) < 64) == (core == 0)
    near_roll = pltpu.roll(near, 64, 1)
    far_roll = pltpu.roll(far, 64, 1)
    even_near = jnp.where(core == 0, near, near_roll)
    even_far = jnp.where(core == 0, far_roll, far)
    odd_near = jnp.where(core == 0, near_roll, near)
    odd_far = jnp.where(core == 0, far, far_roll)
    even_rest = jnp.where(left, even_near, even_far).astype(BF16)
    odd_rest = jnp.where(left, odd_near, odd_far).astype(BF16)
    even = dot_nn(onehot(at == 0), x).astype(BF16)
    odd = dot_nn(onehot(at == HALF), x).astype(BF16)
    for chip in range(CHIPS):
        out_ref[2 * chip, :ROWS] = even
        out_ref[2 * chip, ROWS:] = even_rest
        out_ref[2 * chip + 1, :ROWS] = odd
        out_ref[2 * chip + 1, ROWS:] = odd_rest
    info = dot_nn(onehot(at == 18), x)
    info_ref[...] = jnp.where(core == 0, info, pltpu.roll(info, 64, 1))


def expert_kernel(
    x_ref, info_ref, router_ref, gate_a, gate_b, up_a, up_b, down_a, down_b,
    out_ref, down_v, sem,
):
    expert = lax.axis_index("z") >> 1
    copy = pltpu.make_async_copy(down_b, down_v, sem.at[0])
    copy.start()
    left = iota((ROWS // 2, 128), 1) < 64
    xs = []
    logits = jnp.zeros((ROWS, EXPERTS), F32)
    for g in range(GROUPS):
        parts = []
        for chip in range(g * PER, (g + 1) * PER):
            rest_a = x_ref[2 * chip, ROWS:].astype(F32)
            rest_b = x_ref[2 * chip + 1, ROWS:].astype(F32)
            near = jnp.where(left, rest_a, rest_b)
            far = pltpu.roll(jnp.where(left, rest_b, rest_a), 64, 1)
            middle = jnp.concatenate([near, far], axis=0).astype(BF16)
            parts += [x_ref[2 * chip, :ROWS], middle, x_ref[2 * chip + 1, :ROWS]]
        x = jnp.concatenate(parts, axis=1)
        xs.append(x)
        logits = logits + dot_nt(x, router_ref[:, g * GROUP : (g + 1) * GROUP])
    k = iota((ROWS, EXPERTS), 1)
    named = info_ref[:, :EXPERTS]
    other = jnp.sum(jnp.where((k != expert) & (named > 0.5), logits, 0.0), axis=1, keepdims=True)
    own = jnp.sum(jnp.where(k == expert, logits, 0.0), axis=1, keepdims=True)
    weight = 1.0 / (1.0 + jnp.exp(other - own))
    gate = jnp.zeros((ROWS, UNITS), F32)
    up = jnp.zeros((ROWS, UNITS), F32)
    for g in range(GROUPS):
        rows = slice(g * GROUP, (g + 1) * GROUP)
        x = xs[g]
        gate = gate + dot_nn(x, jnp.concatenate([gate_a[rows, :], gate_b[rows, :]], axis=1))
        up = up + dot_nn(x, jnp.concatenate([up_a[rows, :], up_b[rows, :]], axis=1))
    hidden = (gate / (1.0 + jnp.exp(-gate)) * up * weight).astype(BF16)
    copy.wait()
    for g in range(GROUPS):
        cols = slice(g * GROUP, (g + 1) * GROUP)
        down = jnp.concatenate([down_a[:, cols], down_v[:, cols]], axis=0)
        terms = dot_nn(hidden, down)
        for n in range(PER):
            chip = g * PER + n
            base = n * PAIR
            near = terms[: ROWS // 2, base + 128 : base + 256]
            far = pltpu.roll(terms[ROWS // 2 :, base + 128 : base + 256], 64, 1)
            out_ref[2 * chip, :ROWS] = terms[:, base : base + 128].astype(BF16)
            out_ref[2 * chip, ROWS:] = jnp.where(left, near, far).astype(BF16)
            out_ref[2 * chip + 1, :ROWS] = terms[:, base + 256 : base + 384].astype(BF16)
            out_ref[2 * chip + 1, ROWS:] = jnp.where(left, far, near).astype(BF16)


def share_kernel(in_ref, out_ref):
    core = lax.axis_index("c")
    halves = []
    for half in range(2):
        total = in_ref[half].astype(F32)
        for chip in range(1, CHIPS):
            total = total + in_ref[2 * chip + half].astype(F32)
        halves.append(total)
    even = halves[0][ROWS:]
    odd = halves[1][ROWS:]
    left = iota((ROWS // 2, 128), 1) < 64
    low = jnp.where(left, even, pltpu.roll(odd, 64, 1))
    high = jnp.where(left, pltpu.roll(even, 64, 1), odd)
    near = jnp.where(core == 0, low, high)
    far = jnp.where(core == 0, high, low)
    rest = jnp.concatenate([near, far], axis=0).astype(BF16)
    p = iota((PAYS, ROWS), 1)
    at = iota((PAYS, ROWS), 0) - p - (PAY - HALF) * ((p * 43) >> 8)
    spread = dot_nn(onehot(at == 0), halves[0][:ROWS].astype(BF16))
    spread = spread + dot_nn(onehot(at == HALF), halves[1][:ROWS].astype(BF16))
    spread = spread + dot_nn(onehot(at == 2 * HALF), rest)
    out_ref[...] = spread.reshape(PLANES, PAY, 128).astype(BF16)


def combine_kernel(place_ref, in_ref, out_ref):
    core = lax.axis_index("c")
    x = in_ref[...].astype(F32).reshape(PAYS, 128).astype(BF16)
    side = dot_tn(place_ref[0], x)
    low = dot_tn(place_ref[1], x)
    high = pltpu.roll(dot_tn(place_ref[2], x), 64, 1)
    rest = (low + high)[:, :64]
    even = jnp.concatenate([side, rest], axis=1)
    odd = jnp.concatenate([rest, side], axis=1)
    out_ref[...] = jnp.where(core == 0, even, odd).astype(BF16)


def local(tokens, routes, w_router, w_gate, w_up, w_down):
    swap = [(0, 1), (1, 0)]
    routes_t = routes.T
    payload = pl.pallas_call(
        dispatch_kernel,
        out_shape=jax.ShapeDtypeStruct((PLANES, PAY, 128), BF16),
        in_specs=[vmem(), vmem()],
        out_specs=vmem(),
        name="dispatch",
    )(routes_t, tokens)
    gate_b = lax.ppermute(w_gate, "c", swap)
    up_b = lax.ppermute(w_up, "c", swap)
    down_b = lax.ppermute(w_down, "c", swap)
    place = pl.pallas_call(
        place_kernel,
        out_shape=jax.ShapeDtypeStruct((3, PAYS, TOK), BF16),
        in_specs=[vmem()],
        out_specs=vmem(),
        name="place",
    )(routes_t)
    arrived = lax.all_to_all(payload, "z", 0, 0, tiled=True)
    blocks, info = pl.pallas_call(
        repack_kernel,
        out_shape=(
            jax.ShapeDtypeStruct((2 * CHIPS, PACK, 128), BF16),
            jax.ShapeDtypeStruct((ROWS, 128), F32),
        ),
        in_specs=[vmem()],
        out_specs=(vmem(), vmem()),
        compiler_params=small(),
        cost_estimate=pl.CostEstimate(flops=100000000000, transcendentals=0, bytes_accessed=1048576),
        name="repack",
    )(arrived)
    blocks, place = lax.optimization_barrier((blocks, place))
    gathered = lax.all_to_all(blocks, ("y", "x", "c"), 0, 0, tiled=True)
    terms = pl.pallas_call(
        expert_kernel,
        out_shape=jax.ShapeDtypeStruct((2 * CHIPS, PACK, 128), BF16),
        in_specs=[vmem()] * 8 + [hbm()],
        out_specs=vmem(),
        scratch_shapes=[
            pltpu.VMEM((128, D), BF16),
            pltpu.SemaphoreType.DMA((1,)),
        ],
        compiler_params=pltpu.CompilerParams(vmem_limit_bytes=16 << 20),
        name="expert",
    )(gathered, info, w_router.T, w_gate, gate_b, w_up, up_b, w_down, down_b)
    parts = lax.all_to_all(terms, ("y", "x", "c"), 0, 0, tiled=True)
    shares = pl.pallas_call(
        share_kernel,
        out_shape=jax.ShapeDtypeStruct((PLANES, PAY, 128), BF16),
        in_specs=[vmem()],
        out_specs=vmem(),
        compiler_params=small(),
        name="share",
    )(parts)
    back = lax.all_to_all(shares, "z", 0, 0, tiled=True)
    return pl.pallas_call(
        combine_kernel,
        out_shape=jax.ShapeDtypeStruct((TOK, FEAT), BF16),
        in_specs=[vmem(), vmem()],
        out_specs=vmem(),
        compiler_params=small(),
        name="combine",
    )(place, back)


def solution(mesh):
    fine = Mesh(mesh.devices.reshape(16, 4, 4, 2), ("z", "y", "x", "c"))
    shard = ("y", "x", "c")
    both = ("z",) + shard
    return jax.shard_map(
        local,
        mesh=fine,
        in_specs=(P("z", shard), P("z", None), P(), P(None, both), P(None, both), P(both, None)),
        out_specs=P("z", shard),
        check_vma=False,
    )
```

```python
import jax
import jax.numpy as jnp
from jax import lax
from jax.experimental import pallas as pl
from jax.experimental.pallas import tpu as pltpu
from jax.sharding import Mesh, PartitionSpec as P

EXPERTS = 8
HALF = 6
PLANES = 16
CHIPS = 16
ROWS = PLANES * HALF
TOK = 24
FEAT = 192
PAIR = 384
D = 6144
PAY = 24
PAYS = PLANES * PAY
UNITS = 256
PACK = ROWS + ROWS // 2
PER = 16
GROUPS = CHIPS // PER
GROUP = PER * PAIR
F32 = jnp.float32
BF16 = jnp.bfloat16


def vmem():
    return pl.BlockSpec(memory_space=pltpu.VMEM)


def smem():
    return pl.BlockSpec(memory_space=pltpu.SMEM)


def hbm():
    return pl.BlockSpec(memory_space=pltpu.HBM)


def anyspace():
    return pl.BlockSpec(memory_space=pl.ANY)


def small():
    return pltpu.CompilerParams(vmem_limit_bytes=8 << 20)


def iota(shape, dim):
    return lax.broadcasted_iota(jnp.int32, shape, dim)


def onehot(mask):
    return mask.astype(F32).astype(BF16)


def dot_nt(a, b):
    return lax.dot_general(a, b, (((1,), (1,)), ((), ())), preferred_element_type=F32)


def dot_tn(a, b):
    return lax.dot_general(a, b, (((0,), (0,)), ((), ())), preferred_element_type=F32)


def dot_nn(a, b):
    return jnp.dot(a, b, preferred_element_type=F32)


def ranks(routes_ref):
    first = routes_ref[0:1, :]
    second = routes_ref[1:2, :]
    k8 = iota((EXPERTS, TOK), 0)
    named = onehot((k8 == first) | (k8 == second))
    earlier = onehot(iota((TOK, TOK), 0) < iota((TOK, TOK), 1))
    rank = dot_nn(named, earlier)
    rank = jnp.where(named.astype(F32) > 0.5, rank, 100.0).astype(BF16)
    plane = iota((PLANES, PAY, EXPERTS), 0).reshape(PAYS, EXPERTS)
    pick = onehot((plane >> 1) == iota((PAYS, EXPERTS), 1))
    rank_row = dot_nn(pick, rank)
    i = iota((PLANES, PAY, TOK), 1).reshape(PAYS, TOK)
    return rank_row, i


def dispatch_kernel(routes_ref, tok_ref, out_ref, rank_ref):
    core = lax.axis_index("c")
    rank_row, i = ranks(routes_ref)
    rank_ref[...] = rank_row.astype(BF16)
    first = routes_ref[0:1, :]
    second = routes_ref[1:2, :]
    is_a = i < 12
    is_b = (i >= 12) & (i < 18)
    slot = jnp.where(is_a, i, jnp.where(is_b, i - 12, i - 18))
    hit_low = rank_row == slot.astype(F32)
    hit_high = (rank_row == (slot + HALF).astype(F32)) & (i >= 12)
    tok = tok_ref[...].astype(F32)
    zero = jnp.zeros((TOK, 64), F32)
    part_a = jnp.where(core == 0, tok[:, :128], tok[:, 64:]).astype(BF16)
    head = jnp.concatenate([tok[:, :64], zero], axis=1)
    tail = jnp.concatenate([tok[:, 128:], zero], axis=1)
    part_b = jnp.where(core == 0, tail, head)
    part_b_high = pltpu.roll(part_b, 64, 1).astype(BF16)
    part_b = part_b.astype(BF16)
    lane = iota((128, TOK), 0)
    marks = onehot((lane == first) | (lane == second))
    marks_high = onehot((lane - 64 == first) | (lane - 64 == second))
    payload = dot_nn(onehot(hit_low & is_a), part_a)
    payload = payload + dot_nn(onehot(hit_low & is_b), part_b)
    payload = payload + dot_nn(onehot(hit_high & is_b), part_b_high)
    payload = payload + dot_nt(onehot(hit_low & (i >= 18)), marks)
    payload = payload + dot_nt(onehot(hit_high & (i >= 18)), marks_high)
    out_ref[...] = payload.reshape(PLANES, PAY, 128).astype(BF16)


def repack_kernel(in_ref, out_ref, info_ref):
    core = lax.axis_index("c")
    x = in_ref[...].astype(F32).reshape(PAYS, 128).astype(BF16)
    p = iota((ROWS, PAYS), 0)
    at = iota((ROWS, PAYS), 1) - p - (PAY - HALF) * ((p * 43) >> 8)
    rest = dot_nn(onehot(at == 12), x)
    near = rest[: ROWS // 2]
    far = rest[ROWS // 2 :]
    left = (iota((ROWS // 2, 128), 1) < 64) == (core == 0)
    near_roll = pltpu.roll(near, 64, 1)
    far_roll = pltpu.roll(far, 64, 1)
    even_near = jnp.where(core == 0, near, near_roll)
    even_far = jnp.where(core == 0, far_roll, far)
    odd_near = jnp.where(core == 0, near_roll, near)
    odd_far = jnp.where(core == 0, far, far_roll)
    even_rest = jnp.where(left, even_near, even_far).astype(BF16)
    odd_rest = jnp.where(left, odd_near, odd_far).astype(BF16)
    even = dot_nn(onehot(at == 0), x).astype(BF16)
    odd = dot_nn(onehot(at == HALF), x).astype(BF16)
    for chip in range(CHIPS):
        out_ref[2 * chip, :ROWS] = even
        out_ref[2 * chip, ROWS:] = even_rest
        out_ref[2 * chip + 1, :ROWS] = odd
        out_ref[2 * chip + 1, ROWS:] = odd_rest
    info = dot_nn(onehot(at == 18), x)
    info_ref[...] = jnp.where(core == 0, info, pltpu.roll(info, 64, 1))


def expert_kernel(
    x_ref, info_ref, router_ref, gate_a, gate_b, up_a, up_b, down_a, down_b,
    out_ref, down_v, sem,
):
    expert = lax.axis_index("z") >> 1
    copy = pltpu.make_async_copy(down_b, down_v, sem.at[0])
    copy.start()
    left = iota((ROWS // 2, 128), 1) < 64
    xs = []
    logits = jnp.zeros((ROWS, EXPERTS), F32)
    for g in range(GROUPS):
        parts = []
        for chip in range(g * PER, (g + 1) * PER):
            rest_a = x_ref[2 * chip, ROWS:].astype(F32)
            rest_b = x_ref[2 * chip + 1, ROWS:].astype(F32)
            near = jnp.where(left, rest_a, rest_b)
            far = pltpu.roll(jnp.where(left, rest_b, rest_a), 64, 1)
            middle = jnp.concatenate([near, far], axis=0).astype(BF16)
            parts += [x_ref[2 * chip, :ROWS], middle, x_ref[2 * chip + 1, :ROWS]]
        x = jnp.concatenate(parts, axis=1)
        xs.append(x)
        logits = logits + dot_nt(x, router_ref[:, g * GROUP : (g + 1) * GROUP])
    k = iota((ROWS, EXPERTS), 1)
    named = info_ref[:, :EXPERTS]
    other = jnp.sum(jnp.where((k != expert) & (named > 0.5), logits, 0.0), axis=1, keepdims=True)
    own = jnp.sum(jnp.where(k == expert, logits, 0.0), axis=1, keepdims=True)
    weight = 1.0 / (1.0 + jnp.exp(other - own))
    gate = jnp.zeros((ROWS, UNITS), F32)
    up = jnp.zeros((ROWS, UNITS), F32)
    for g in range(GROUPS):
        rows = slice(g * GROUP, (g + 1) * GROUP)
        x = xs[g]
        gate = gate + dot_nn(x, jnp.concatenate([gate_a[rows, :], gate_b[rows, :]], axis=1))
        up = up + dot_nn(x, jnp.concatenate([up_a[rows, :], up_b[rows, :]], axis=1))
    hidden = (gate / (1.0 + jnp.exp(-gate)) * up * weight).astype(BF16)
    copy.wait()
    for g in range(GROUPS):
        cols = slice(g * GROUP, (g + 1) * GROUP)
        down = jnp.concatenate([down_a[:, cols], down_v[:, cols]], axis=0)
        terms = dot_nn(hidden, down)
        for n in range(PER):
            chip = g * PER + n
            base = n * PAIR
            near = terms[: ROWS // 2, base + 128 : base + 256]
            far = pltpu.roll(terms[ROWS // 2 :, base + 128 : base + 256], 64, 1)
            out_ref[2 * chip, :ROWS] = terms[:, base : base + 128].astype(BF16)
            out_ref[2 * chip, ROWS:] = jnp.where(left, near, far).astype(BF16)
            out_ref[2 * chip + 1, :ROWS] = terms[:, base + 256 : base + 384].astype(BF16)
            out_ref[2 * chip + 1, ROWS:] = jnp.where(left, far, near).astype(BF16)


def share_kernel(in_ref, out_ref):
    core = lax.axis_index("c")
    halves = []
    for half in range(2):
        total = in_ref[half].astype(F32)
        for chip in range(1, CHIPS):
            total = total + in_ref[2 * chip + half].astype(F32)
        halves.append(total)
    even = halves[0][ROWS:]
    odd = halves[1][ROWS:]
    left = iota((ROWS // 2, 128), 1) < 64
    low = jnp.where(left, even, pltpu.roll(odd, 64, 1))
    high = jnp.where(left, pltpu.roll(even, 64, 1), odd)
    near = jnp.where(core == 0, low, high)
    far = jnp.where(core == 0, high, low)
    rest = jnp.concatenate([near, far], axis=0).astype(BF16)
    p = iota((PAYS, ROWS), 1)
    at = iota((PAYS, ROWS), 0) - p - (PAY - HALF) * ((p * 43) >> 8)
    spread = dot_nn(onehot(at == 0), halves[0][:ROWS].astype(BF16))
    spread = spread + dot_nn(onehot(at == HALF), halves[1][:ROWS].astype(BF16))
    spread = spread + dot_nn(onehot(at == 2 * HALF), rest)
    out_ref[...] = spread.reshape(PLANES, PAY, 128).astype(BF16)


def combine_kernel(rank_ref, in_ref, out_ref):
    core = lax.axis_index("c")
    x = in_ref[...].astype(F32).reshape(PAYS, 128).astype(BF16)
    rank = rank_ref[...].astype(F32)
    i = iota((PLANES, PAY, TOK), 1).reshape(PAYS, TOK)
    inside = (i >= 12) & (i < 18)
    side = dot_tn(onehot((rank == i.astype(F32)) & (i < 12)), x)
    low = dot_tn(onehot((rank == (i - 12).astype(F32)) & inside), x)
    high = dot_tn(onehot((rank == (i - 12 + HALF).astype(F32)) & inside), x)
    high = pltpu.roll(high, 64, 1)
    rest = (low + high)[:, :64]
    even = jnp.concatenate([side, rest], axis=1)
    odd = jnp.concatenate([rest, side], axis=1)
    out_ref[...] = jnp.where(core == 0, even, odd).astype(BF16)


def local(tokens, routes, w_router, w_gate, w_up, w_down):
    swap = [(0, 1), (1, 0)]
    routes_t = routes.T
    payload, rank = pl.pallas_call(
        dispatch_kernel,
        out_shape=(
            jax.ShapeDtypeStruct((PLANES, PAY, 128), BF16),
            jax.ShapeDtypeStruct((PAYS, TOK), BF16),
        ),
        in_specs=[vmem(), vmem()],
        out_specs=(vmem(), vmem()),
        name="dispatch",
    )(routes_t, tokens)
    gate_b = lax.ppermute(w_gate, "c", swap)
    up_b = lax.ppermute(w_up, "c", swap)
    down_b = lax.ppermute(w_down, "c", swap)
    arrived = lax.all_to_all(payload, "z", 0, 0, tiled=True)
    blocks, info = pl.pallas_call(
        repack_kernel,
        out_shape=(
            jax.ShapeDtypeStruct((2 * CHIPS, PACK, 128), BF16),
            jax.ShapeDtypeStruct((ROWS, 128), F32),
        ),
        in_specs=[vmem()],
        out_specs=(vmem(), vmem()),
        compiler_params=small(),
        cost_estimate=pl.CostEstimate(flops=100000000000, transcendentals=0, bytes_accessed=1048576),
        name="repack",
    )(arrived)
    gathered = lax.all_to_all(blocks, ("y", "x", "c"), 0, 0, tiled=True)
    terms = pl.pallas_call(
        expert_kernel,
        out_shape=jax.ShapeDtypeStruct((2 * CHIPS, PACK, 128), BF16),
        in_specs=[vmem()] * 8 + [hbm()],
        out_specs=vmem(),
        scratch_shapes=[
            pltpu.VMEM((128, D), BF16),
            pltpu.SemaphoreType.DMA((1,)),
        ],
        compiler_params=pltpu.CompilerParams(vmem_limit_bytes=16 << 20),
        name="expert",
    )(gathered, info, w_router.T, w_gate, gate_b, w_up, up_b, w_down, down_b)
    parts = lax.all_to_all(terms, ("y", "x", "c"), 0, 0, tiled=True)
    shares = pl.pallas_call(
        share_kernel,
        out_shape=jax.ShapeDtypeStruct((PLANES, PAY, 128), BF16),
        in_specs=[vmem()],
        out_specs=vmem(),
        compiler_params=small(),
        name="share",
    )(parts)
    back = lax.all_to_all(shares, "z", 0, 0, tiled=True)
    return pl.pallas_call(
        combine_kernel,
        out_shape=jax.ShapeDtypeStruct((TOK, FEAT), BF16),
        in_specs=[vmem(), vmem()],
        out_specs=vmem(),
        compiler_params=small(),
        name="combine",
    )(rank, back)


def solution(mesh):
    fine = Mesh(mesh.devices.reshape(16, 4, 4, 2), ("z", "y", "x", "c"))
    shard = ("y", "x", "c")
    both = ("z",) + shard
    return jax.shard_map(
        local,
        mesh=fine,
        in_specs=(P("z", shard), P("z", None), P(), P(None, both), P(None, both), P(both, None)),
        out_specs=P("z", shard),
        check_vma=False,
    )
```

```python
import jax
import jax.numpy as jnp
from jax import lax
from jax.experimental import pallas as pl
from jax.experimental.pallas import tpu as pltpu
from jax.sharding import Mesh, PartitionSpec as P

EXPERTS = 8
HALF = 6
PLANES = 16
CHIPS = 16
ROWS = PLANES * HALF
TOK = 24
FEAT = 192
PAIR = 384
D = 6144
PAY = 20
PAYS = PLANES * PAY
BACK = 18
BACKS = PLANES * BACK
UNITS = 256
PACK = ROWS + ROWS // 2
PER = 16
GROUPS = CHIPS // PER
GROUP = PER * PAIR
F32 = jnp.float32
BF16 = jnp.bfloat16


def vmem():
    return pl.BlockSpec(memory_space=pltpu.VMEM)


def smem():
    return pl.BlockSpec(memory_space=pltpu.SMEM)


def hbm():
    return pl.BlockSpec(memory_space=pltpu.HBM)


def anyspace():
    return pl.BlockSpec(memory_space=pl.ANY)


def small():
    return pltpu.CompilerParams(vmem_limit_bytes=8 << 20)


def iota(shape, dim):
    return lax.broadcasted_iota(jnp.int32, shape, dim)


def onehot(mask):
    return mask.astype(F32).astype(BF16)


def dot_nt(a, b):
    return lax.dot_general(a, b, (((1,), (1,)), ((), ())), preferred_element_type=F32)


def dot_tn(a, b):
    return lax.dot_general(a, b, (((0,), (0,)), ((), ())), preferred_element_type=F32)


def dot_nn(a, b):
    return jnp.dot(a, b, preferred_element_type=F32)


def ranks(routes_ref):
    first = routes_ref[0:1, :]
    second = routes_ref[1:2, :]
    k8 = iota((EXPERTS, TOK), 0)
    named = onehot((k8 == first) | (k8 == second))
    earlier = onehot(iota((TOK, TOK), 0) < iota((TOK, TOK), 1))
    rank = dot_nn(named, earlier)
    return jnp.where(named.astype(F32) > 0.5, rank, 100.0).astype(BF16)


def dispatch_kernel(routes_ref, tok_ref, out_ref, rank_ref):
    core = lax.axis_index("c")
    rank = ranks(routes_ref)
    row = iota((PAYS, EXPERTS), 0)
    plane = (row * 205) >> 12
    mine = (plane >> 1) == iota((PAYS, EXPERTS), 1)
    rank_row = dot_nn(onehot(mine), rank)
    row = iota((PAYS, TOK), 0)
    i = row - PAY * ((row * 205) >> 12)
    tok = tok_ref[...].astype(F32)
    zero = jnp.zeros((TOK, 64), F32)
    part_a = jnp.where(core == 0, tok[:, :128], tok[:, 64:]).astype(BF16)
    head = jnp.concatenate([tok[:, :64], zero], axis=1)
    tail = jnp.concatenate([tok[:, 128:], zero], axis=1)
    part_b = jnp.where(core == 0, tail, head)
    part_b_high = pltpu.roll(part_b, 64, 1).astype(BF16)
    part_b = part_b.astype(BF16)
    payload = dot_nn(onehot((rank_row == i.astype(F32)) & (i < 12)), part_a)
    rest = (i >= 12) & (i < 18)
    payload = payload + dot_nn(onehot((rank_row == (i - 12).astype(F32)) & rest), part_b)
    rest_high = (rank_row == (i - 12 + HALF).astype(F32)) & rest
    payload = payload + dot_nn(onehot(rest_high), part_b_high)
    first = routes_ref[0:1, :]
    second = routes_ref[1:2, :]
    k8 = iota((EXPERTS, TOK), 0)
    named = onehot((k8 == first) | (k8 == second))
    lane = iota((EXPERTS, 128), 1)
    named_lane = dot_tn(named, onehot((lane & 7) == iota((EXPERTS, 128), 0)))
    rank_col = dot_tn(rank, onehot(iota((EXPERTS, EXPERTS), 0) == iota((EXPERTS, EXPERTS), 1)))
    slot = (iota((TOK, 128), 1) >> 3).astype(F32)
    marks = [
        jnp.sum(jnp.where(rank_col[:, k : k + 1] == slot, named_lane, 0.0), axis=0, keepdims=True)
        for k in range(EXPERTS)
    ]
    marks = jnp.concatenate(marks, axis=0).astype(BF16)
    at = iota((PAYS, EXPERTS), 0) - PAY * plane
    payload = payload + dot_nn(onehot(mine & (at == 18)), marks)
    out_ref[...] = payload.astype(BF16)
    plane = (iota((BACKS, EXPERTS), 0) * 57) >> 10
    rank_ref[...] = dot_nn(onehot((plane >> 1) == iota((BACKS, EXPERTS), 1)), rank).astype(BF16)


def repack_kernel(in_ref, out_ref, info_ref):
    core = lax.axis_index("c")
    x = in_ref[...]
    p = iota((ROWS, PAYS), 0)
    home = (p * 43) >> 8
    col = iota((ROWS, PAYS), 1)
    at = col - p - (PAY - HALF) * home
    rest = dot_nn(onehot(at == 12), x)
    near = rest[: ROWS // 2]
    far = rest[ROWS // 2 :]
    left = (iota((ROWS // 2, 128), 1) < 64) == (core == 0)
    near_roll = pltpu.roll(near, 64, 1)
    far_roll = pltpu.roll(far, 64, 1)
    even_near = jnp.where(core == 0, near, near_roll)
    even_far = jnp.where(core == 0, far_roll, far)
    odd_near = jnp.where(core == 0, near_roll, near)
    odd_far = jnp.where(core == 0, far, far_roll)
    even_rest = jnp.where(left, even_near, even_far).astype(BF16)
    odd_rest = jnp.where(left, odd_near, odd_far).astype(BF16)
    even = dot_nn(onehot(at == 0), x).astype(BF16)
    odd = dot_nn(onehot(at == HALF), x).astype(BF16)
    for chip in range(CHIPS):
        out_ref[2 * chip, :ROWS] = even
        out_ref[2 * chip, ROWS:] = even_rest
        out_ref[2 * chip + 1, :ROWS] = odd
        out_ref[2 * chip + 1, ROWS:] = odd_rest
    marks = dot_nn(onehot(col - PAY * home == 18), x)
    p = iota((ROWS, 128), 0)
    slot = p - HALF * ((p * 43) >> 8) + HALF * core
    marks = jnp.where((iota((ROWS, 128), 1) >> 3) == slot, marks, 0.0).astype(BF16)
    info_ref[...] = dot_nn(marks, onehot((iota((128, 128), 0) & 7) == iota((128, 128), 1)))


def expert_kernel(
    x_ref, info_ref, router_ref, gate_a, gate_b, up_a, up_b, down_a, down_b,
    out_ref, down_v, sem,
):
    expert = lax.axis_index("z") >> 1
    copy = pltpu.make_async_copy(down_b, down_v, sem.at[0])
    copy.start()
    left = iota((ROWS // 2, 128), 1) < 64
    xs = []
    logits = jnp.zeros((ROWS, EXPERTS), F32)
    for g in range(GROUPS):
        parts = []
        for chip in range(g * PER, (g + 1) * PER):
            rest_a = x_ref[2 * chip, ROWS:].astype(F32)
            rest_b = x_ref[2 * chip + 1, ROWS:].astype(F32)
            near = jnp.where(left, rest_a, rest_b)
            far = pltpu.roll(jnp.where(left, rest_b, rest_a), 64, 1)
            middle = jnp.concatenate([near, far], axis=0).astype(BF16)
            parts += [x_ref[2 * chip, :ROWS], middle, x_ref[2 * chip + 1, :ROWS]]
        x = jnp.concatenate(parts, axis=1)
        xs.append(x)
        logits = logits + dot_nt(x, router_ref[:, g * GROUP : (g + 1) * GROUP])
    k = iota((ROWS, EXPERTS), 1)
    named = info_ref[:, :EXPERTS]
    other = jnp.sum(jnp.where((k != expert) & (named > 0.5), logits, 0.0), axis=1, keepdims=True)
    own = jnp.sum(jnp.where(k == expert, logits, 0.0), axis=1, keepdims=True)
    weight = 1.0 / (1.0 + jnp.exp(other - own))
    gate = jnp.zeros((ROWS, UNITS), F32)
    up = jnp.zeros((ROWS, UNITS), F32)
    for g in range(GROUPS):
        rows = slice(g * GROUP, (g + 1) * GROUP)
        x = xs[g]
        gate = gate + dot_nn(x, jnp.concatenate([gate_a[rows, :], gate_b[rows, :]], axis=1))
        up = up + dot_nn(x, jnp.concatenate([up_a[rows, :], up_b[rows, :]], axis=1))
    hidden = (gate / (1.0 + jnp.exp(-gate)) * up * weight).astype(BF16)
    copy.wait()
    for g in range(GROUPS):
        cols = slice(g * GROUP, (g + 1) * GROUP)
        down = jnp.concatenate([down_a[:, cols], down_v[:, cols]], axis=0)
        terms = dot_nn(hidden, down)
        for n in range(PER):
            chip = g * PER + n
            base = n * PAIR
            near = terms[: ROWS // 2, base + 128 : base + 256]
            far = pltpu.roll(terms[ROWS // 2 :, base + 128 : base + 256], 64, 1)
            out_ref[2 * chip, :ROWS] = terms[:, base : base + 128].astype(BF16)
            out_ref[2 * chip, ROWS:] = jnp.where(left, near, far).astype(BF16)
            out_ref[2 * chip + 1, :ROWS] = terms[:, base + 256 : base + 384].astype(BF16)
            out_ref[2 * chip + 1, ROWS:] = jnp.where(left, far, near).astype(BF16)


def share_kernel(in_ref, out_ref):
    core = lax.axis_index("c")
    halves = []
    for half in range(2):
        total = in_ref[half].astype(F32)
        for chip in range(1, CHIPS):
            total = total + in_ref[2 * chip + half].astype(F32)
        halves.append(total)
    even = halves[0][ROWS:]
    odd = halves[1][ROWS:]
    left = iota((ROWS // 2, 128), 1) < 64
    low = jnp.where(left, even, pltpu.roll(odd, 64, 1))
    high = jnp.where(left, pltpu.roll(even, 64, 1), odd)
    near = jnp.where(core == 0, low, high)
    far = jnp.where(core == 0, high, low)
    rest = jnp.concatenate([near, far], axis=0).astype(BF16)
    p = iota((BACKS, ROWS), 1)
    at = iota((BACKS, ROWS), 0) - p - (BACK - HALF) * ((p * 43) >> 8)
    spread = dot_nn(onehot(at == 0), halves[0][:ROWS].astype(BF16))
    spread = spread + dot_nn(onehot(at == HALF), halves[1][:ROWS].astype(BF16))
    spread = spread + dot_nn(onehot(at == 2 * HALF), rest)
    out_ref[...] = spread.astype(BF16)


def combine_kernel(rank_ref, in_ref, out_ref):
    core = lax.axis_index("c")
    x = in_ref[...]
    rank = rank_ref[...].astype(F32)
    row = iota((BACKS, TOK), 0)
    i = row - BACK * ((row * 57) >> 10)
    side = dot_tn(onehot((rank == i.astype(F32)) & (i < 12)), x)
    low = dot_tn(onehot((rank == (i - 12).astype(F32)) & (i >= 12)), x)
    high = dot_tn(onehot((rank == (i - 12 + HALF).astype(F32)) & (i >= 12)), x)
    high = pltpu.roll(high, 64, 1)
    rest = (low + high)[:, :64]
    even = jnp.concatenate([side, rest], axis=1)
    odd = jnp.concatenate([rest, side], axis=1)
    out_ref[...] = jnp.where(core == 0, even, odd).astype(BF16)


def local(tokens, routes, w_router, w_gate, w_up, w_down):
    swap = [(0, 1), (1, 0)]
    routes_t = routes.T
    payload, rank = pl.pallas_call(
        dispatch_kernel,
        out_shape=(
            jax.ShapeDtypeStruct((PAYS, 128), BF16),
            jax.ShapeDtypeStruct((BACKS, TOK), BF16),
        ),
        in_specs=[vmem(), vmem()],
        out_specs=(vmem(), vmem()),
        name="dispatch",
    )(routes_t, tokens)
    gate_b = lax.ppermute(w_gate, "c", swap)
    up_b = lax.ppermute(w_up, "c", swap)
    down_b = lax.ppermute(w_down, "c", swap)
    payload = payload.reshape(PLANES, PAY // 2, 2, 128)
    arrived = lax.all_to_all(payload, "z", 0, 0, tiled=True).reshape(PAYS, 128)
    blocks, info = pl.pallas_call(
        repack_kernel,
        out_shape=(
            jax.ShapeDtypeStruct((2 * CHIPS, PACK, 128), BF16),
            jax.ShapeDtypeStruct((ROWS, 128), F32),
        ),
        in_specs=[vmem()],
        out_specs=(vmem(), vmem()),
        compiler_params=small(),
        cost_estimate=pl.CostEstimate(flops=100000000000, transcendentals=0, bytes_accessed=1048576),
        name="repack",
    )(arrived)
    gathered = lax.all_to_all(blocks, ("y", "x", "c"), 0, 0, tiled=True)
    terms = pl.pallas_call(
        expert_kernel,
        out_shape=jax.ShapeDtypeStruct((2 * CHIPS, PACK, 128), BF16),
        in_specs=[vmem()] * 8 + [hbm()],
        out_specs=vmem(),
        scratch_shapes=[
            pltpu.VMEM((128, D), BF16),
            pltpu.SemaphoreType.DMA((1,)),
        ],
        compiler_params=pltpu.CompilerParams(vmem_limit_bytes=16 << 20),
        name="expert",
    )(gathered, info, w_router.T, w_gate, gate_b, w_up, up_b, w_down, down_b)
    parts = lax.all_to_all(terms, ("y", "x", "c"), 0, 0, tiled=True)
    shares = pl.pallas_call(
        share_kernel,
        out_shape=jax.ShapeDtypeStruct((BACKS, 128), BF16),
        in_specs=[vmem()],
        out_specs=vmem(),
        compiler_params=small(),
        name="share",
    )(parts)
    shares = shares.reshape(PLANES, BACK // 2, 2, 128)
    back = lax.all_to_all(shares, "z", 0, 0, tiled=True).reshape(BACKS, 128)
    return pl.pallas_call(
        combine_kernel,
        out_shape=jax.ShapeDtypeStruct((TOK, FEAT), BF16),
        in_specs=[vmem(), vmem()],
        out_specs=vmem(),
        compiler_params=small(),
        name="combine",
    )(rank, back)


def solution(mesh):
    fine = Mesh(mesh.devices.reshape(16, 4, 4, 2), ("z", "y", "x", "c"))
    shard = ("y", "x", "c")
    both = ("z",) + shard
    return jax.shard_map(
        local,
        mesh=fine,
        in_specs=(P("z", shard), P("z", None), P(), P(None, both), P(None, both), P(both, None)),
        out_specs=P("z", shard),
        check_vma=False,
    )
```

```python
import jax
import jax.numpy as jnp
from jax import lax
from jax.experimental import pallas as pl
from jax.experimental.pallas import tpu as pltpu
from jax.sharding import Mesh, PartitionSpec as P

EXPERTS = 8
HALF = 6
PLANES = 16
CHIPS = 16
ROWS = PLANES * HALF
TOK = 24
FEAT = 192
PAIR = 384
D = 6144
PAY = 20
PAYS = PLANES * PAY
BACK = 18
BACKS = PLANES * BACK
UNITS = 256
PACK = ROWS + ROWS // 2
PER = 16
GROUPS = CHIPS // PER
GROUP = PER * PAIR
F32 = jnp.float32
BF16 = jnp.bfloat16


def vmem():
    return pl.BlockSpec(memory_space=pltpu.VMEM)


def hbm():
    return pl.BlockSpec(memory_space=pltpu.HBM)


def small():
    return pltpu.CompilerParams(vmem_limit_bytes=8 << 20)


def iota(shape, dim):
    return lax.broadcasted_iota(jnp.int32, shape, dim)


def onehot(mask):
    return mask.astype(F32).astype(BF16)


def dot_nt(a, b):
    return lax.dot_general(a, b, (((1,), (1,)), ((), ())), preferred_element_type=F32)


def dot_tn(a, b):
    return lax.dot_general(a, b, (((0,), (0,)), ((), ())), preferred_element_type=F32)


def dot_nn(a, b):
    return jnp.dot(a, b, preferred_element_type=F32)


def ranks(routes_ref):
    first = routes_ref[0:1, :]
    second = routes_ref[1:2, :]
    k8 = iota((EXPERTS, TOK), 0)
    named = onehot((k8 == first) | (k8 == second))
    earlier = onehot(iota((TOK, TOK), 0) < iota((TOK, TOK), 1))
    rank = dot_nn(named, earlier)
    return jnp.where(named.astype(F32) > 0.5, rank, 100.0).astype(BF16)


def dispatch_kernel(routes_ref, tok_ref, out_ref, rank_ref):
    core = lax.axis_index("c")
    rank = ranks(routes_ref)
    row = iota((PAYS, EXPERTS), 0)
    plane = (row * 205) >> 12
    mine = (plane >> 1) == iota((PAYS, EXPERTS), 1)
    rank_row = dot_nn(onehot(mine), rank)
    row = iota((PAYS, TOK), 0)
    i = row - PAY * ((row * 205) >> 12)
    tok = tok_ref[...].astype(F32)
    zero = jnp.zeros((TOK, 64), F32)
    part_a = jnp.where(core == 0, tok[:, :128], tok[:, 64:]).astype(BF16)
    head = jnp.concatenate([tok[:, :64], zero], axis=1)
    tail = jnp.concatenate([tok[:, 128:], zero], axis=1)
    part_b = jnp.where(core == 0, tail, head)
    part_b_high = pltpu.roll(part_b, 64, 1).astype(BF16)
    part_b = part_b.astype(BF16)
    payload = dot_nn(onehot((rank_row == i.astype(F32)) & (i < 12)), part_a)
    rest = (i >= 12) & (i < 18)
    payload = payload + dot_nn(onehot((rank_row == (i - 12).astype(F32)) & rest), part_b)
    rest_high = (rank_row == (i - 12 + HALF).astype(F32)) & rest
    payload = payload + dot_nn(onehot(rest_high), part_b_high)
    first = routes_ref[0:1, :]
    second = routes_ref[1:2, :]
    k8 = iota((EXPERTS, TOK), 0)
    named = onehot((k8 == first) | (k8 == second))
    lane = iota((EXPERTS, 128), 1)
    named_lane = dot_tn(named, onehot((lane & 7) == iota((EXPERTS, 128), 0)))
    rank_col = dot_tn(rank, onehot(iota((EXPERTS, EXPERTS), 0) == iota((EXPERTS, EXPERTS), 1)))
    slot = (iota((TOK, 128), 1) >> 3).astype(F32)
    marks = [
        jnp.sum(jnp.where(rank_col[:, k : k + 1] == slot, named_lane, 0.0), axis=0, keepdims=True)
        for k in range(EXPERTS)
    ]
    marks = jnp.concatenate(marks, axis=0).astype(BF16)
    at = iota((PAYS, EXPERTS), 0) - PAY * plane
    payload = payload + dot_nn(onehot(mine & (at == 18)), marks)
    out_ref[...] = payload.astype(BF16)
    plane = (iota((EXPERTS, BACKS), 1) * 57) >> 10
    pick = onehot((plane >> 1) == iota((EXPERTS, BACKS), 0))
    rank_ref[...] = dot_tn(rank, pick).astype(BF16)


def repack_kernel(in_ref, out_ref, info_ref):
    core = lax.axis_index("c")
    x = in_ref[...]
    p = iota((ROWS, PAYS), 0)
    home = (p * 43) >> 8
    col = iota((ROWS, PAYS), 1)
    at = col - p - (PAY - HALF) * home
    rest = dot_nn(onehot(at == 12), x)
    near = rest[: ROWS // 2]
    far = rest[ROWS // 2 :]
    left = (iota((ROWS // 2, 128), 1) < 64) == (core == 0)
    near_roll = pltpu.roll(near, 64, 1)
    far_roll = pltpu.roll(far, 64, 1)
    even_near = jnp.where(core == 0, near, near_roll)
    even_far = jnp.where(core == 0, far_roll, far)
    odd_near = jnp.where(core == 0, near_roll, near)
    odd_far = jnp.where(core == 0, far, far_roll)
    even_rest = jnp.where(left, even_near, even_far).astype(BF16)
    odd_rest = jnp.where(left, odd_near, odd_far).astype(BF16)
    even = dot_nn(onehot(at == 0), x).astype(BF16)
    odd = dot_nn(onehot(at == HALF), x).astype(BF16)
    for chip in range(CHIPS):
        out_ref[2 * chip, :ROWS] = even
        out_ref[2 * chip, ROWS:] = even_rest
        out_ref[2 * chip + 1, :ROWS] = odd
        out_ref[2 * chip + 1, ROWS:] = odd_rest
    marks = dot_nn(onehot(col - PAY * home == 18), x)
    p = iota((ROWS, 128), 0)
    slot = p - HALF * ((p * 43) >> 8) + HALF * core
    marks = jnp.where((iota((ROWS, 128), 1) >> 3) == slot, marks, 0.0).astype(BF16)
    info_ref[...] = dot_nn(marks, onehot((iota((128, 128), 0) & 7) == iota((128, 128), 1)))


def expert_kernel(
    x_ref, info_ref, router_ref, gate_a, gate_b, up_a, up_b, down_a, down_b,
    out_ref, down_v, sem,
):
    expert = lax.axis_index("z") >> 1
    copy = pltpu.make_async_copy(down_b, down_v, sem.at[0])
    copy.start()
    left = iota((ROWS // 2, 128), 1) < 64
    xs = []
    logits = jnp.zeros((ROWS, EXPERTS), F32)
    for g in range(GROUPS):
        parts = []
        for chip in range(g * PER, (g + 1) * PER):
            rest_a = x_ref[2 * chip, ROWS:].astype(F32)
            rest_b = x_ref[2 * chip + 1, ROWS:].astype(F32)
            near = jnp.where(left, rest_a, rest_b)
            far = pltpu.roll(jnp.where(left, rest_b, rest_a), 64, 1)
            middle = jnp.concatenate([near, far], axis=0).astype(BF16)
            parts += [x_ref[2 * chip, :ROWS], middle, x_ref[2 * chip + 1, :ROWS]]
        x = jnp.concatenate(parts, axis=1)
        xs.append(x)
        logits = logits + dot_nt(x, router_ref[:, g * GROUP : (g + 1) * GROUP])
    k = iota((ROWS, EXPERTS), 1)
    named = info_ref[:, :EXPERTS]
    other = jnp.sum(jnp.where((k != expert) & (named > 0.5), logits, 0.0), axis=1, keepdims=True)
    own = jnp.sum(jnp.where(k == expert, logits, 0.0), axis=1, keepdims=True)
    weight = 1.0 / (1.0 + jnp.exp(other - own))
    gate = jnp.zeros((ROWS, UNITS), F32)
    up = jnp.zeros((ROWS, UNITS), F32)
    for g in range(GROUPS):
        rows = slice(g * GROUP, (g + 1) * GROUP)
        x = xs[g]
        gate = gate + dot_nn(x, jnp.concatenate([gate_a[rows, :], gate_b[rows, :]], axis=1))
        up = up + dot_nn(x, jnp.concatenate([up_a[rows, :], up_b[rows, :]], axis=1))
    hidden = (gate / (1.0 + jnp.exp(-gate)) * up * weight).astype(BF16)
    copy.wait()
    for g in range(GROUPS):
        cols = slice(g * GROUP, (g + 1) * GROUP)
        down = jnp.concatenate([down_a[:, cols], down_v[:, cols]], axis=0)
        terms = dot_nn(hidden, down)
        for n in range(PER):
            chip = g * PER + n
            base = n * PAIR
            near = terms[: ROWS // 2, base + 128 : base + 256]
            far = pltpu.roll(terms[ROWS // 2 :, base + 128 : base + 256], 64, 1)
            out_ref[2 * chip, :ROWS] = terms[:, base : base + 128].astype(BF16)
            out_ref[2 * chip, ROWS:] = jnp.where(left, near, far).astype(BF16)
            out_ref[2 * chip + 1, :ROWS] = terms[:, base + 256 : base + 384].astype(BF16)
            out_ref[2 * chip + 1, ROWS:] = jnp.where(left, far, near).astype(BF16)


def share_kernel(in_ref, out_ref):
    core = lax.axis_index("c")
    halves = []
    for half in range(2):
        total = in_ref[half].astype(F32)
        for chip in range(1, CHIPS):
            total = total + in_ref[2 * chip + half].astype(F32)
        halves.append(total)
    even = halves[0][ROWS:]
    odd = halves[1][ROWS:]
    left = iota((ROWS // 2, 128), 1) < 64
    low = jnp.where(left, even, pltpu.roll(odd, 64, 1))
    high = jnp.where(left, pltpu.roll(even, 64, 1), odd)
    near = jnp.where(core == 0, low, high)
    far = jnp.where(core == 0, high, low)
    rest = jnp.concatenate([near, far], axis=0).astype(BF16)
    p = iota((BACKS, ROWS), 1)
    at = iota((BACKS, ROWS), 0) - p - (BACK - HALF) * ((p * 43) >> 8)
    spread = dot_nn(onehot(at == 0), halves[0][:ROWS].astype(BF16))
    spread = spread + dot_nn(onehot(at == HALF), halves[1][:ROWS].astype(BF16))
    spread = spread + dot_nn(onehot(at == 2 * HALF), rest)
    out_ref[...] = spread.astype(BF16)


def combine_kernel(rank_ref, in_ref, out_ref):
    core = lax.axis_index("c")
    x = in_ref[...]
    rank = rank_ref[...].astype(F32)
    row = iota((TOK, BACKS), 1)
    i = row - BACK * ((row * 57) >> 10)
    side = dot_nn(onehot((rank == i.astype(F32)) & (i < 12)), x)
    low = dot_nn(onehot((rank == (i - 12).astype(F32)) & (i >= 12)), x)
    high = dot_nn(onehot((rank == (i - 12 + HALF).astype(F32)) & (i >= 12)), x)
    high = pltpu.roll(high, 64, 1)
    rest = (low + high)[:, :64]
    even = jnp.concatenate([side, rest], axis=1)
    odd = jnp.concatenate([rest, side], axis=1)
    out_ref[...] = jnp.where(core == 0, even, odd).astype(BF16)


def local(tokens, routes, w_router, w_gate, w_up, w_down):
    swap = [(0, 1), (1, 0)]
    routes_t = routes.T
    payload, rank = pl.pallas_call(
        dispatch_kernel,
        out_shape=(
            jax.ShapeDtypeStruct((PAYS, 128), BF16),
            jax.ShapeDtypeStruct((TOK, BACKS), BF16),
        ),
        in_specs=[vmem(), vmem()],
        out_specs=(vmem(), vmem()),
        name="dispatch",
    )(routes_t, tokens)
    gate_b = lax.ppermute(w_gate, "c", swap)
    up_b = lax.ppermute(w_up, "c", swap)
    down_b = lax.ppermute(w_down, "c", swap)
    payload = payload.reshape(PLANES, PAY // 2, 2, 128)
    arrived = lax.all_to_all(payload, "z", 0, 0, tiled=True).reshape(PAYS, 128)
    blocks, info = pl.pallas_call(
        repack_kernel,
        out_shape=(
            jax.ShapeDtypeStruct((2 * CHIPS, PACK, 128), BF16),
            jax.ShapeDtypeStruct((ROWS, 128), F32),
        ),
        in_specs=[vmem()],
        out_specs=(vmem(), vmem()),
        compiler_params=small(),
        cost_estimate=pl.CostEstimate(flops=100000000000, transcendentals=0, bytes_accessed=1048576),
        name="repack",
    )(arrived)
    gathered = lax.all_to_all(blocks, ("y", "x", "c"), 0, 0, tiled=True)
    terms = pl.pallas_call(
        expert_kernel,
        out_shape=jax.ShapeDtypeStruct((2 * CHIPS, PACK, 128), BF16),
        in_specs=[vmem()] * 8 + [hbm()],
        out_specs=vmem(),
        scratch_shapes=[
            pltpu.VMEM((128, D), BF16),
            pltpu.SemaphoreType.DMA((1,)),
        ],
        compiler_params=pltpu.CompilerParams(vmem_limit_bytes=16 << 20),
        name="expert",
    )(gathered, info, w_router.T, w_gate, gate_b, w_up, up_b, w_down, down_b)
    parts = lax.all_to_all(terms, ("y", "x", "c"), 0, 0, tiled=True)
    shares = pl.pallas_call(
        share_kernel,
        out_shape=jax.ShapeDtypeStruct((BACKS, 128), BF16),
        in_specs=[vmem()],
        out_specs=vmem(),
        compiler_params=small(),
        name="share",
    )(parts)
    shares = shares.reshape(PLANES, BACK // 2, 2, 128)
    back = lax.all_to_all(shares, "z", 0, 0, tiled=True).reshape(BACKS, 128)
    return pl.pallas_call(
        combine_kernel,
        out_shape=jax.ShapeDtypeStruct((TOK, FEAT), BF16),
        in_specs=[vmem(), vmem()],
        out_specs=vmem(),
        compiler_params=small(),
        name="combine",
    )(rank, back)


def solution(mesh):
    fine = Mesh(mesh.devices.reshape(16, 4, 4, 2), ("z", "y", "x", "c"))
    shard = ("y", "x", "c")
    both = ("z",) + shard
    return jax.shard_map(
        local,
        mesh=fine,
        in_specs=(P("z", shard), P("z", None), P(), P(None, both), P(None, both), P(both, None)),
        out_specs=P("z", shard),
        check_vma=False,
    )
```

```python
import jax
import jax.numpy as jnp
from jax import lax
from jax.experimental import pallas as pl
from jax.experimental.pallas import tpu as pltpu
from jax.sharding import Mesh, PartitionSpec as P

EXPERTS = 8
HALF = 6
PLANES = 16
CHIPS = 16
ROWS = PLANES * HALF
TOK = 24
FEAT = 192
PAIR = 384
D = 6144
PAY = 20
PAYS = PLANES * PAY
BACK = 18
BACKS = PLANES * BACK
UNITS = 256
PACK = ROWS + ROWS // 2
PER = 16
GROUPS = CHIPS // PER
GROUP = PER * PAIR
F32 = jnp.float32
BF16 = jnp.bfloat16


def vmem():
    return pl.BlockSpec(memory_space=pltpu.VMEM)


def hbm():
    return pl.BlockSpec(memory_space=pltpu.HBM)


def small():
    return pltpu.CompilerParams(vmem_limit_bytes=8 << 20)


def iota(shape, dim):
    return lax.broadcasted_iota(jnp.int32, shape, dim)


def onehot(mask):
    return mask.astype(F32).astype(BF16)


def dot_nt(a, b):
    return lax.dot_general(a, b, (((1,), (1,)), ((), ())), preferred_element_type=F32)


def dot_tn(a, b):
    return lax.dot_general(a, b, (((0,), (0,)), ((), ())), preferred_element_type=F32)


def dot_nn(a, b):
    return jnp.dot(a, b, preferred_element_type=F32)


def ranks(routes_ref):
    first = routes_ref[0:1, :]
    second = routes_ref[1:2, :]
    k8 = iota((EXPERTS, TOK), 0)
    named = onehot((k8 == first) | (k8 == second))
    earlier = onehot(iota((TOK, TOK), 0) < iota((TOK, TOK), 1))
    rank = dot_nn(named, earlier)
    return jnp.where(named.astype(F32) > 0.5, rank, 100.0).astype(BF16)


def dispatch_kernel(routes_ref, tok_ref, out_ref, rank_ref):
    core = lax.axis_index("c")
    rank = ranks(routes_ref)
    row = iota((PAYS, EXPERTS), 0)
    plane = (row * 205) >> 12
    mine = (plane >> 1) == iota((PAYS, EXPERTS), 1)
    rank_row = dot_nn(onehot(mine), rank)
    row = iota((PAYS, TOK), 0)
    i = row - PAY * ((row * 205) >> 12)
    tok = tok_ref[...].astype(F32)
    zero = jnp.zeros((TOK, 64), F32)
    part_a = jnp.where(core == 0, tok[:, :128], tok[:, 64:]).astype(BF16)
    head = jnp.concatenate([tok[:, :64], zero], axis=1)
    tail = jnp.concatenate([tok[:, 128:], zero], axis=1)
    part_b = jnp.where(core == 0, tail, head)
    part_b_high = pltpu.roll(part_b, 64, 1).astype(BF16)
    part_b = part_b.astype(BF16)
    payload = dot_nn(onehot((rank_row == i.astype(F32)) & (i < 12)), part_a)
    rest = (i >= 12) & (i < 18)
    payload = payload + dot_nn(onehot((rank_row == (i - 12).astype(F32)) & rest), part_b)
    rest_high = (rank_row == (i - 12 + HALF).astype(F32)) & rest
    payload = payload + dot_nn(onehot(rest_high), part_b_high)
    first = routes_ref[0:1, :]
    second = routes_ref[1:2, :]
    k8 = iota((EXPERTS, TOK), 0)
    named = onehot((k8 == first) | (k8 == second))
    lane = iota((EXPERTS, 128), 1)
    named_lane = dot_tn(named, onehot((lane & 7) == iota((EXPERTS, 128), 0)))
    same = onehot(iota((EXPERTS, EXPERTS), 0) == iota((EXPERTS, EXPERTS), 1))
    count_col = dot_nt(onehot(iota((TOK, TOK), 1) < iota((TOK, TOK), 0)), named)
    rank_col = jnp.where(dot_tn(named, same) > 0.5, count_col, 100.0)
    slot = (iota((TOK, 128), 1) >> 3).astype(F32)
    marks = [
        jnp.sum(jnp.where(rank_col[:, k : k + 1] == slot, named_lane, 0.0), axis=0, keepdims=True)
        for k in range(EXPERTS)
    ]
    marks = jnp.concatenate(marks, axis=0).astype(BF16)
    at = iota((PAYS, EXPERTS), 0) - PAY * plane
    payload = payload + dot_nn(onehot(mine & (at == 18)), marks)
    out_ref[...] = payload.astype(BF16)
    plane = (iota((EXPERTS, BACKS), 1) * 57) >> 10
    pick = onehot((plane >> 1) == iota((EXPERTS, BACKS), 0))
    rank_ref[...] = dot_tn(rank, pick).astype(BF16)


def repack_kernel(in_ref, out_ref, info_ref):
    core = lax.axis_index("c")
    x = in_ref[...]
    p = iota((ROWS, PAYS), 0)
    home = (p * 43) >> 8
    col = iota((ROWS, PAYS), 1)
    at = col - p - (PAY - HALF) * home
    rest = dot_nn(onehot(at == 12), x)
    near = rest[: ROWS // 2]
    far = rest[ROWS // 2 :]
    left = (iota((ROWS // 2, 128), 1) < 64) == (core == 0)
    near_roll = pltpu.roll(near, 64, 1)
    far_roll = pltpu.roll(far, 64, 1)
    even_near = jnp.where(core == 0, near, near_roll)
    even_far = jnp.where(core == 0, far_roll, far)
    odd_near = jnp.where(core == 0, near_roll, near)
    odd_far = jnp.where(core == 0, far, far_roll)
    even_rest = jnp.where(left, even_near, even_far).astype(BF16)
    odd_rest = jnp.where(left, odd_near, odd_far).astype(BF16)
    even = dot_nn(onehot(at == 0), x).astype(BF16)
    odd = dot_nn(onehot(at == HALF), x).astype(BF16)
    for chip in range(CHIPS):
        out_ref[2 * chip, :ROWS] = even
        out_ref[2 * chip, ROWS:] = even_rest
        out_ref[2 * chip + 1, :ROWS] = odd
        out_ref[2 * chip + 1, ROWS:] = odd_rest
    marks = dot_nn(onehot(col - PAY * home == 18), x)
    p = iota((ROWS, 128), 0)
    slot = p - HALF * ((p * 43) >> 8) + HALF * core
    marks = jnp.where((iota((ROWS, 128), 1) >> 3) == slot, marks, 0.0).astype(BF16)
    info_ref[...] = dot_nn(marks, onehot((iota((128, 128), 0) & 7) == iota((128, 128), 1)))


def expert_kernel(
    x_ref, info_ref, router_ref, gate_a, gate_b, up_a, up_b, down_a, down_b,
    out_ref, down_v, sem,
):
    expert = lax.axis_index("z") >> 1
    copy = pltpu.make_async_copy(down_b, down_v, sem.at[0])
    copy.start()
    left = iota((ROWS // 2, 128), 1) < 64
    xs = []
    logits = jnp.zeros((ROWS, EXPERTS), F32)
    for g in range(GROUPS):
        parts = []
        for chip in range(g * PER, (g + 1) * PER):
            rest_a = x_ref[2 * chip, ROWS:].astype(F32)
            rest_b = x_ref[2 * chip + 1, ROWS:].astype(F32)
            near = jnp.where(left, rest_a, rest_b)
            far = pltpu.roll(jnp.where(left, rest_b, rest_a), 64, 1)
            middle = jnp.concatenate([near, far], axis=0).astype(BF16)
            parts += [x_ref[2 * chip, :ROWS], middle, x_ref[2 * chip + 1, :ROWS]]
        x = jnp.concatenate(parts, axis=1)
        xs.append(x)
        logits = logits + dot_nt(x, router_ref[:, g * GROUP : (g + 1) * GROUP])
    k = iota((ROWS, EXPERTS), 1)
    named = info_ref[:, :EXPERTS]
    other = jnp.sum(jnp.where((k != expert) & (named > 0.5), logits, 0.0), axis=1, keepdims=True)
    own = jnp.sum(jnp.where(k == expert, logits, 0.0), axis=1, keepdims=True)
    weight = 1.0 / (1.0 + jnp.exp(other - own))
    gate = jnp.zeros((ROWS, UNITS), F32)
    up = jnp.zeros((ROWS, UNITS), F32)
    for g in range(GROUPS):
        rows = slice(g * GROUP, (g + 1) * GROUP)
        x = xs[g]
        gate = gate + dot_nn(x, jnp.concatenate([gate_a[rows, :], gate_b[rows, :]], axis=1))
        up = up + dot_nn(x, jnp.concatenate([up_a[rows, :], up_b[rows, :]], axis=1))
    hidden = (gate / (1.0 + jnp.exp(-gate)) * up * weight).astype(BF16)
    copy.wait()
    for g in range(GROUPS):
        cols = slice(g * GROUP, (g + 1) * GROUP)
        down = jnp.concatenate([down_a[:, cols], down_v[:, cols]], axis=0)
        terms = dot_nn(hidden, down)
        for n in range(PER):
            chip = g * PER + n
            base = n * PAIR
            near = terms[: ROWS // 2, base + 128 : base + 256]
            far = pltpu.roll(terms[ROWS // 2 :, base + 128 : base + 256], 64, 1)
            out_ref[2 * chip, :ROWS] = terms[:, base : base + 128].astype(BF16)
            out_ref[2 * chip, ROWS:] = jnp.where(left, near, far).astype(BF16)
            out_ref[2 * chip + 1, :ROWS] = terms[:, base + 256 : base + 384].astype(BF16)
            out_ref[2 * chip + 1, ROWS:] = jnp.where(left, far, near).astype(BF16)


def share_kernel(in_ref, out_ref):
    core = lax.axis_index("c")
    halves = []
    for half in range(2):
        total = in_ref[half].astype(F32)
        for chip in range(1, CHIPS):
            total = total + in_ref[2 * chip + half].astype(F32)
        halves.append(total)
    even = halves[0][ROWS:]
    odd = halves[1][ROWS:]
    left = iota((ROWS // 2, 128), 1) < 64
    low = jnp.where(left, even, pltpu.roll(odd, 64, 1))
    high = jnp.where(left, pltpu.roll(even, 64, 1), odd)
    near = jnp.where(core == 0, low, high)
    far = jnp.where(core == 0, high, low)
    rest = jnp.concatenate([near, far], axis=0).astype(BF16)
    p = iota((BACKS, ROWS), 1)
    at = iota((BACKS, ROWS), 0) - p - (BACK - HALF) * ((p * 43) >> 8)
    spread = dot_nn(onehot(at == 0), halves[0][:ROWS].astype(BF16))
    spread = spread + dot_nn(onehot(at == HALF), halves[1][:ROWS].astype(BF16))
    spread = spread + dot_nn(onehot(at == 2 * HALF), rest)
    out_ref[...] = spread.astype(BF16)


def combine_kernel(rank_ref, in_ref, out_ref):
    core = lax.axis_index("c")
    x = in_ref[...]
    rank = rank_ref[...].astype(F32)
    row = iota((TOK, BACKS), 1)
    i = row - BACK * ((row * 57) >> 10)
    side = dot_nn(onehot((rank == i.astype(F32)) & (i < 12)), x)
    low = dot_nn(onehot((rank == (i - 12).astype(F32)) & (i >= 12)), x)
    high = dot_nn(onehot((rank == (i - 12 + HALF).astype(F32)) & (i >= 12)), x)
    high = pltpu.roll(high, 64, 1)
    rest = (low + high)[:, :64]
    even = jnp.concatenate([side, rest], axis=1)
    odd = jnp.concatenate([rest, side], axis=1)
    out_ref[...] = jnp.where(core == 0, even, odd).astype(BF16)


def local(tokens, routes, w_router, w_gate, w_up, w_down):
    swap = [(0, 1), (1, 0)]
    routes_t = routes.T
    payload, rank = pl.pallas_call(
        dispatch_kernel,
        out_shape=(
            jax.ShapeDtypeStruct((PAYS, 128), BF16),
            jax.ShapeDtypeStruct((TOK, BACKS), BF16),
        ),
        in_specs=[vmem(), vmem()],
        out_specs=(vmem(), vmem()),
        name="dispatch",
    )(routes_t, tokens)
    gate_b = lax.ppermute(w_gate, "c", swap)
    up_b = lax.ppermute(w_up, "c", swap)
    down_b = lax.ppermute(w_down, "c", swap)
    payload = payload.reshape(PLANES, PAY // 2, 2, 128)
    arrived = lax.all_to_all(payload, "z", 0, 0, tiled=True).reshape(PAYS, 128)
    blocks, info = pl.pallas_call(
        repack_kernel,
        out_shape=(
            jax.ShapeDtypeStruct((2 * CHIPS, PACK, 128), BF16),
            jax.ShapeDtypeStruct((ROWS, 128), F32),
        ),
        in_specs=[vmem()],
        out_specs=(vmem(), vmem()),
        compiler_params=small(),
        cost_estimate=pl.CostEstimate(flops=100000000000, transcendentals=0, bytes_accessed=1048576),
        name="repack",
    )(arrived)
    gathered = lax.all_to_all(blocks, ("y", "x", "c"), 0, 0, tiled=True)
    terms = pl.pallas_call(
        expert_kernel,
        out_shape=jax.ShapeDtypeStruct((2 * CHIPS, PACK, 128), BF16),
        in_specs=[vmem()] * 8 + [hbm()],
        out_specs=vmem(),
        scratch_shapes=[
            pltpu.VMEM((128, D), BF16),
            pltpu.SemaphoreType.DMA((1,)),
        ],
        compiler_params=pltpu.CompilerParams(vmem_limit_bytes=16 << 20),
        name="expert",
    )(gathered, info, w_router.T, w_gate, gate_b, w_up, up_b, w_down, down_b)
    parts = lax.all_to_all(terms, ("y", "x", "c"), 0, 0, tiled=True)
    shares = pl.pallas_call(
        share_kernel,
        out_shape=jax.ShapeDtypeStruct((BACKS, 128), BF16),
        in_specs=[vmem()],
        out_specs=vmem(),
        compiler_params=small(),
        name="share",
    )(parts)
    shares = shares.reshape(PLANES, BACK // 2, 2, 128)
    back = lax.all_to_all(shares, "z", 0, 0, tiled=True).reshape(BACKS, 128)
    return pl.pallas_call(
        combine_kernel,
        out_shape=jax.ShapeDtypeStruct((TOK, FEAT), BF16),
        in_specs=[vmem(), vmem()],
        out_specs=vmem(),
        compiler_params=small(),
        name="combine",
    )(rank, back)


def solution(mesh):
    fine = Mesh(mesh.devices.reshape(16, 4, 4, 2), ("z", "y", "x", "c"))
    shard = ("y", "x", "c")
    both = ("z",) + shard
    return jax.shard_map(
        local,
        mesh=fine,
        in_specs=(P("z", shard), P("z", None), P(), P(None, both), P(None, both), P(both, None)),
        out_specs=P("z", shard),
        check_vma=False,
    )
```
